32 devices in a mesh: dp: 4 (over y, x), shard: 8 (over z, core).
Axes of the slice: x: 2, y: 2, z: 4, core: 2. Of those that a mesh axis runs over, the one named last changes fastest.
Arguments:
- layer_input: bfloat16 [384, 46240], P('shard', 'dp'), may hold values from -6 to 6
- cotangent: bfloat16 [32768, 512], P('dp'), may hold values from -0.032958984 to 0.032958984
- momentum: float32 [10368, 512], P('shard'), may hold values from -6 to 6
Outputs:
- momentum_new: float32 [10368, 512], P('shard')
- direction: float32 [10368, 512], P('shard')
The draws below stay inside these ranges and needn't reach their ends.
All inputs are finite; a program needn't handle non-finite values.
Results may differ from the reference program's by a relative error of at most 0.0003.
Values sent between devices are 32-bit elements; how exact they have to be, the bound alone decides.
No kernel may reach another device: no remote copies, remote signals or barrier semaphores. Data moves between devices by JAX's collectives and lax.ppermute only.
A program may use at most 320 MiB of HBM per device.

```python
import jax
import jax.numpy as jnp
from jax import lax

CIN = 384
COUT = 512
HW = 32
DEPTH = 8
ITERS = 2
VOXELS = 32768
ROWS = 10368
N_DP = 4


def steps_of(rng, extent, pieces, low, top_value):
    def one(dim, shards_of):
        heights = jax.random.uniform(jax.random.fold_in(jax.random.fold_in(rng, 6), dim), (shards_of,), jnp.float32, low / len(pieces), top_value / len(pieces))
        return jnp.repeat(jnp.exp(heights), extent[dim] // shards_of).reshape((-1,) + (1,) * (len(extent) - dim - 1))

    factor_of = one(*pieces[0])
    for cut in pieces[1:]:
        factor_of = factor_of * one(*cut)
    return factor_of


def bell_draw(key, dims, width, bound, pieces=(), kind=jnp.bfloat16):
    array = width * jax.random.normal(key, dims, jnp.float32)
    if pieces:
        array = array * steps_of(key, dims, pieces, -0.22, 0.18)
    return jnp.clip(array, -bound, bound).astype(kind)


def setup_inputs(seed: int = 0) -> dict:
    key_list = jax.random.split(jax.random.key(seed), 4)
    return {
        "layer_input": bell_draw(key_list[0], (CIN, N_DP * (DEPTH + 2) * (HW + 2) * (HW + 2)), 1.0, 6.0, ((0, 8), (1, 4))),
        "cotangent": bell_draw(key_list[1], (VOXELS, COUT), (VOXELS ** -0.5), 0.032958984, ((0, 4),)),
        "momentum": bell_draw(key_list[2], (ROWS, COUT), 1.0, 6.0, ((0, 8),), jnp.float32),
    }


HIGH = lax.Precision.HIGHEST

def build_patches(volume):
    slabs = []
    for kd in range(3):
        for kh in range(3):
            for kw in range(3):
                slabs.append(volume[:, kd:kd + DEPTH, kh:kh + HW, kw:kw + HW])
    stacked = jnp.stack(slabs, axis=1)
    return stacked.reshape(CIN * 27, DEPTH * HW * HW)

def reference(layer_input, cotangent, momentum):
    volumes = layer_input.reshape(CIN, N_DP, DEPTH + 2, HW + 2, HW + 2)
    volumes = jnp.moveaxis(volumes, 1, 0)
    cotans = cotangent.reshape(N_DP, DEPTH * HW * HW, COUT)

    def accumulate(total, pair):
        volume, cotan = pair
        patches = build_patches(volume)
        return (total + jnp.dot(patches, cotan, preferred_element_type=jnp.float32), None)
    start = jnp.zeros((CIN * 27, COUT), jnp.float32)
    grad, unused = lax.scan(accumulate, start, (volumes, cotans))
    momentum_new = 0.95 * momentum + grad
    iterate = momentum_new / (jnp.sqrt(jnp.sum(momentum_new * momentum_new)) + 1e-07)
    for step in range(ITERS):
        gram = jnp.dot(iterate.T, iterate, precision=HIGH)
        poly = -4.775 * gram + 2.0315 * jnp.dot(gram, gram, precision=HIGH)
        iterate = 3.4445 * iterate + jnp.dot(iterate, poly, precision=HIGH)
    direction = iterate * jnp.sqrt(jnp.float32(27 * CIN))
    return (momentum_new, direction)
```

```python
import functools

import jax
import jax.numpy as jnp
from jax import lax
from jax.experimental import pallas as pl
from jax.experimental.pallas import tpu as pltpu
from jax.sharding import PartitionSpec as P

HW = 32
ROWS = 10368
PW = HW + 2
LANE = 128
TAPS = 27
A1, B1, C1 = 3.4445, -4.775, 2.0315
F32 = jnp.float32
BF16 = jnp.bfloat16
VMEM = pl.BlockSpec(memory_space=pltpu.VMEM)
HBM = pl.BlockSpec(memory_space=pl.ANY)
SMEM = pl.BlockSpec(memory_space=pltpu.SMEM)
BLOCKS = (((0, 0), (0, 1), (0, 2), (0, 3), (1, 1)), ((1, 2), (1, 3), (2, 2), (2, 3), (3, 3)))


def column(rows):
    return pl.BlockSpec((rows, LANE), lambda c: (0, c))


def params():
    return pltpu.CompilerParams(vmem_limit_bytes=56 << 20)


def pair(tile, p, lane):
    t, c = divmod(p, LANE)
    if c + 64 <= LANE:
        return jnp.where(lane < c + 32, tile(t), tile(t + 4))
    if c + 32 <= LANE:
        far = jnp.where(lane < c, tile(t + 5), tile(t))
        if c + 32 == LANE:
            return far
        return jnp.where(lane < c + 32, far, tile(t + 4))
    near = jnp.where(lane < c + 32 - LANE, tile(t + 1), tile(t + 5))
    return jnp.where(lane < c, near, tile(t))


def build_slab(d0, half, xs, tail, v, cp):
    lane = lax.broadcasted_iota(jnp.int32, (16, LANE), 1)
    last = xs.shape[1] // LANE
    for g in range(cp // 16):
        rows = slice(16 * g, 16 * g + 16)

        def tile(t):
            return tail[rows, :] if t == last else xs[rows, LANE * t : LANE * t + LANE]

        for j in range(18):
            for kw in range(3):
                part = []
                for s1 in range(2):
                    p = (d0 + half * s1) * PW * PW + PW * j + kw
                    part.append(pltpu.roll(pair(tile, p, lane), (64 * s1 - p) % LANE, 1))
                r0 = (d0 * 3 + kw) * cp + 16 * g
                v[r0 : r0 + 16, LANE * j : LANE * j + LANE] = jnp.where(lane < 64, part[0], part[1])


def conv_kernel(depth, cp, taps, slots, q_ref, x_hbm, cot_hbm, *refs):
    outs = refs[:2]
    xs, tail, cot, v, xsem, csem = refs[2:]
    half = depth // 2
    ln = xs.shape[1]
    vox = HW * HW
    xcopy = pltpu.make_async_copy(x_hbm, xs, xsem)
    xcopy.start()
    copies = []
    for i in range(depth):
        rows = pl.ds(i * vox, vox)
        copies.append(pltpu.make_async_copy(cot_hbm.at[rows], cot.at[rows], csem.at[i]))
    for d in range(half):
        for s1 in range(2):
            copies[d + half * s1].start()
    xcopy.wait()
    n = ln // LANE * LANE
    if n < ln:
        tail[:, : ln - n] = xs[:, n:]
    for d0 in range(half + 2):
        build_slab(d0, half, xs, tail, v, cp)
    for d in range(half):
        for s1 in range(2):
            copies[d + half * s1].wait()
        for c in range(2):
            lhs = []
            for s in range(slots):
                for i in range(taps):
                    t = jnp.minimum(q_ref[slots * c + s] * taps + i, TAPS - 1)
                    kd, kh, kw = t // 9, t // 3 % 3, t % 3
                    r0 = pl.multiple_of(((d + kd) * 3 + kw) * cp, 16)
                    lhs.append(v[pl.ds(r0, cp), pl.ds(pl.multiple_of(LANE * kh, LANE), 16 * LANE)])
            rhs = []
            for h in range(16):
                for s1 in range(2):
                    for s0 in range(2):
                        r0 = (d + half * s1) * vox + (h + 16 * s0) * HW
                        rhs.append(cot[r0 : r0 + HW, 256 * c : 256 * c + 256])
            part = jnp.dot(jnp.concatenate(lhs, 0), jnp.concatenate(rhs, 0), preferred_element_type=F32)
            if d == 0:
                outs[c][...] = part
            else:
                outs[c][...] += part


def conv(x, cot, q, taps, slots):
    cp, ln = x.shape
    depth = cot.shape[0] // (HW * HW)
    return pl.pallas_call(
        functools.partial(conv_kernel, depth, cp, taps, slots),
        out_shape=[jax.ShapeDtypeStruct((slots * taps * cp, 256), F32)] * 2,
        in_specs=[SMEM, HBM, HBM],
        out_specs=[VMEM] * 2,
        scratch_shapes=[
            pltpu.VMEM((cp, ln), BF16),
            pltpu.VMEM((cp, LANE), BF16),
            pltpu.VMEM(cot.shape, BF16),
            pltpu.VMEM((3 * (depth // 2 + 2) * cp, 18 * LANE), BF16),
            pltpu.SemaphoreType.DMA,
            pltpu.SemaphoreType.DMA((depth,)),
        ],
        compiler_params=params(),
        name="conv_wgrad",
    )(q, x, cot)


def own_kernel(taps, cp, dp_ref, m_ref, o_ref):
    chans = m_ref.shape[0] // TAPS
    for i in range(taps):
        t = dp_ref[0] * taps + i
        rows = m_ref[pl.ds(jnp.minimum(t, TAPS - 1), chans, stride=TAPS), :]
        o_ref[cp * i : cp * i + chans, :] = jnp.where(t < TAPS, rows, 0.0)
        if cp > chans:
            o_ref[cp * i + chans : cp * i + cp, :] = jnp.zeros((cp - chans, LANE), F32)


def own_momentum(momentum, dp, taps, cp):
    return pl.pallas_call(
        functools.partial(own_kernel, taps, cp),
        out_shape=jax.ShapeDtypeStruct((taps * cp, momentum.shape[1]), F32),
        grid=(momentum.shape[1] // LANE,),
        in_specs=[SMEM, column(momentum.shape[0])],
        out_specs=column(taps * cp),
        compiler_params=params(),
        name="own_momentum",
    )(dp, momentum)


def split(x):
    hi = x.astype(BF16)
    return hi, (x - hi.astype(F32)).astype(BF16)


def dot_t(a, b):
    return lax.dot_general(a, b, (((0,), (0,)), ((), ())), preferred_element_type=F32)


def update(m_ref, grad, dp, taps, cp):
    rows = taps * cp
    tap = dp * taps + lax.broadcasted_iota(jnp.int32, (rows, 1), 0) // cp
    return jnp.where(tap < TAPS, 0.95 * m_ref[...] + grad, 0.0)


def upper_gram(m):
    hi, lo = split(m)
    out = []
    for i in range(4):
        a, b = slice(128 * i, 128 * i + 128), slice(128 * i, 512)
        out.append(dot_t(hi[:, a], hi[:, b]) + (dot_t(hi[:, a], lo[:, b]) + dot_t(lo[:, a], hi[:, b])))
    return out


def step_kernel(taps, cp, dp_ref, m_ref, a0, ra, a2, b0, rb, b2, o_ref, keep, send):
    rows = taps * cp
    dp, core = dp_ref[0], dp_ref[1]
    ga = a0[:rows] + ra[:rows] + a2[...]
    gb = b0[:rows] + rb[:rows] + b2[...]
    m = update(m_ref, jnp.concatenate([ga, gb], 1), dp, taps, cp)
    o_ref[...] = m
    gram = upper_gram(m)
    for half in range(2):
        mine = core == half
        for n, (i, j) in enumerate(BLOCKS[half]):
            block = gram[i][:, 128 * (j - i) : 128 * (j - i) + 128]
            for r in range(4):
                piece = block[32 * r : 32 * r + 32]

                @pl.when(mine)
                def _():
                    keep[r ^ dp, n] = piece

                @pl.when(jnp.logical_not(mine))
                def _():
                    send[r ^ dp, n] = piece


def step(dp, own, pieces, taps, cp):
    g = jax.ShapeDtypeStruct((4, 5, 32, 128), F32)
    return pl.pallas_call(
        functools.partial(step_kernel, taps, cp),
        out_shape=[jax.ShapeDtypeStruct(own.shape, F32), g, g],
        in_specs=[SMEM] + [VMEM] * 7,
        out_specs=[VMEM] * 3,
        compiler_params=params(),
        name="momentum_gram",
    )(dp, own, *pieces)


def any_step_kernel(taps, cp, dp_ref, m_ref, grad, o_ref, g_ref):
    m = update(m_ref, grad[...], dp_ref[0], taps, cp)
    o_ref[...] = m
    for i, rows in enumerate(upper_gram(m)):
        g_ref[128 * i : 128 * i + 128, :] = jnp.zeros((128, 512), F32)
        g_ref[128 * i : 128 * i + 128, 128 * i :] = rows


def any_step(dp, own, grad, taps, cp):
    return pl.pallas_call(
        functools.partial(any_step_kernel, taps, cp),
        out_shape=[jax.ShapeDtypeStruct(own.shape, F32), jax.ShapeDtypeStruct((512, 512), F32)],
        in_specs=[SMEM, VMEM, VMEM],
        out_specs=[VMEM] * 2,
        compiler_params=params(),
        name="momentum_gram",
    )(dp, own, grad)


def order_kernel(taps, cp, chans, dp_ref, *refs):
    o_ref = refs[-1]
    for r, ref in enumerate(refs[:-1]):
        for i in range(ref.shape[0] // cp):
            t = (dp_ref[0] ^ r) * taps + i if len(refs) > 2 else i
            if len(refs) == 2 and i >= TAPS:
                continue

            @pl.when(t < TAPS)
            def _():
                o_ref[pl.ds(t, chans, stride=TAPS), :] = ref[cp * i : cp * i + chans, :]


def order(dp, parts, taps, cp, chans):
    return pl.pallas_call(
        functools.partial(order_kernel, taps, cp, chans),
        out_shape=jax.ShapeDtypeStruct((chans * TAPS, parts[0].shape[1]), F32),
        grid=(parts[0].shape[1] // LANE,),
        in_specs=[SMEM] + [column(part.shape[0]) for part in parts],
        out_specs=column(chans * TAPS),
        compiler_params=params(),
        name="weight_order",
    )(dp, *parts)


def mm(a, b):
    ah, al = a
    bh, bl = b
    d = functools.partial(jnp.dot, preferred_element_type=F32)
    return d(ah, bh) + (d(ah, bl) + d(al, bh))


def apply_kernel(dp_ref, m_ref, *refs):
    parts, (o_ref, g_ref) = refs[:-2], refs[-2:]
    if len(parts) == 1:
        g_ref[...] = parts[0][...]
    else:
        dp, core = dp_ref[0], dp_ref[1]
        for n, part in enumerate(parts):
            which, r = divmod(n, 4)
            q = dp ^ r
            for half in range(2):

                @pl.when(core ^ which == half)
                def _():
                    for k, (i, j) in enumerate(BLOCKS[half]):
                        rows = pl.ds(pl.multiple_of(128 * i + 32 * q, 32), 32)
                        g_ref[rows, 128 * j : 128 * j + 128] = part[k]

    for i in range(4):
        for j in range(i + 1, 4):
            g_ref[128 * j : 128 * j + 128, 128 * i : 128 * i + 128] = g_ref[
                128 * i : 128 * i + 128, 128 * j : 128 * j + 128
            ].T
    gram = g_ref[...]
    n = gram.shape[0]
    diag = lax.broadcasted_iota(jnp.int32, (n, n), 0) == lax.broadcasted_iota(jnp.int32, (n, n), 1)
    trace = jnp.sum(jnp.where(diag, gram, 0.0), keepdims=True)
    scale = 1.0 / (jnp.sqrt(trace) + 1e-07)
    g = gram * scale * scale
    gs = split(g)
    p1 = jnp.where(diag, A1, 0.0) + B1 * g + C1 * mm(gs, gs)
    p1s = split(p1)
    g2 = mm(split(mm(gs, p1s)), p1s)
    g2s = split(g2)
    p2 = jnp.where(diag, A1, 0.0) + B1 * g2 + C1 * mm(g2s, g2s)
    qs = split(mm(p1s, split(p2)) * (scale * jnp.sqrt(F32(ROWS))))
    o_ref[...] = mm(split(m_ref[...]), qs)


def apply(dp, momentum_new, parts):
    return pl.pallas_call(
        apply_kernel,
        out_shape=jax.ShapeDtypeStruct(momentum_new.shape, F32),
        in_specs=[SMEM] + [VMEM] * (1 + len(parts)),
        out_specs=VMEM,
        scratch_shapes=[pltpu.VMEM((512, 512), F32)],
        compiler_params=params(),
        name="newton_schulz",
    )(dp, momentum_new, *parts)


def swap(x, axis, size, bit):
    return lax.ppermute(x, axis, [(i, i ^ bit) for i in range(size)])


def body_4x8(layer_input, cotangent, momentum):
    chans = momentum.shape[0] // TAPS
    cp = layer_input.shape[0]
    taps = 7
    dp = lax.axis_index("dp")
    ids = jnp.stack([dp, lax.axis_index("shard") % 2]).astype(jnp.int32)
    first = jnp.stack([dp ^ 1, dp ^ 3, dp ^ 2, dp ^ 3]).astype(jnp.int32)
    second = jnp.stack([dp, dp ^ 2, dp, dp ^ 1]).astype(jnp.int32)
    rows = taps * cp
    sa, sb = conv(layer_input, cotangent, first, taps, 2)
    ra = swap(sa, "dp", 4, 1)
    rb = swap(sb, "dp", 4, 2)
    ka, kb = conv(layer_input, cotangent, second, taps, 2)
    own = own_momentum(momentum, ids, taps, cp)
    a2 = swap(ra[rows:] + ka[rows:], "dp", 4, 2)
    b2 = swap(rb[rows:] + kb[rows:], "dp", 4, 1)
    mine, keep, send = step(ids, own, (ka, ra, a2, kb, rb, b2), taps, cp)
    got = swap(send, "shard", 8, 1)
    others = [swap(mine, "dp", 4, r) for r in (1, 2, 3)]
    g = keep + got
    g = g[0] + swap(g[1], "dp", 4, 1) + swap(g[2], "dp", 4, 2) + swap(g[3], "dp", 4, 3)
    g = g + swap(g, "shard", 8, 2) + swap(g, "shard", 8, 4) + swap(g, "shard", 8, 6)
    g = [g] + [swap(g, "dp", 4, r) for r in (1, 2, 3)]
    g = g + [swap(x, "shard", 8, 1) for x in g]
    momentum_new = order(ids, [mine] + others, taps, cp, chans)
    return momentum_new, apply(ids, momentum_new, g)


def body_any(n_dp, layer_input, cotangent, momentum):
    chans = layer_input.shape[0]
    cp = -(-chans // 16) * 16
    taps = -(-TAPS // n_dp)
    x = jnp.pad(layer_input, ((0, cp - chans), (0, 0)))
    ids = jnp.stack([lax.axis_index("dp"), lax.axis_index("shard")]).astype(jnp.int32)
    q = jnp.tile(jnp.arange(n_dp, dtype=jnp.int32), 2)
    part = jnp.concatenate(conv(x, cotangent, q, taps, n_dp), 1)
    grad = lax.psum_scatter(part, "dp", scatter_dimension=0, tiled=True)
    mine, gram = any_step(ids, own_momentum(momentum, ids, taps, cp), grad, taps, cp)
    gram = lax.psum(gram, ("dp", "shard"))
    momentum_new = order(ids, [lax.all_gather(mine, "dp", axis=0, tiled=True)], taps, cp, chans)
    return momentum_new, apply(ids, momentum_new, [gram])


def solution(mesh):
    n_dp = mesh.shape["dp"]
    known = (n_dp, mesh.shape["shard"]) == (4, 8)
    return jax.shard_map(
        body_4x8 if known else functools.partial(body_any, n_dp),
        mesh=mesh,
        in_specs=(P("shard", "dp"), P("dp", None), P("shard", None)),
        out_specs=(P("shard", None), P("shard", None)),
        check_vma=False,
    )
```

```python
import functools

import jax
import jax.numpy as jnp
from jax import lax
from jax.experimental import pallas as pl
from jax.experimental.pallas import tpu as pltpu
from jax.sharding import PartitionSpec as P

HW = 32
ROWS = 10368
PW = HW + 2
LANE = 128
TAPS = 27
A1, B1, C1 = 3.4445, -4.775, 2.0315
F32 = jnp.float32
BF16 = jnp.bfloat16
VMEM = pl.BlockSpec(memory_space=pltpu.VMEM)
HBM = pl.BlockSpec(memory_space=pl.ANY)
BLOCKS = (((0, 0), (0, 1), (0, 2), (0, 3), (1, 1)), ((1, 2), (1, 3), (2, 2), (2, 3), (3, 3)))


def column(rows):
    return pl.BlockSpec((rows, LANE), lambda c: (0, c))


def params(mib=24):
    return pltpu.CompilerParams(vmem_limit_bytes=mib << 20)


def near(x):
    return pltpu.with_memory_space_constraint(x, pltpu.VMEM)


def pair(tile, p, lane):
    t, c = divmod(p, LANE)
    if c + 64 <= LANE:
        return jnp.where(lane < c + 32, tile(t), tile(t + 4))
    if c + 32 <= LANE:
        far = jnp.where(lane < c, tile(t + 5), tile(t))
        if c + 32 == LANE:
            return far
        return jnp.where(lane < c + 32, far, tile(t + 4))
    near = jnp.where(lane < c + 32 - LANE, tile(t + 1), tile(t + 5))
    return jnp.where(lane < c, near, tile(t))


def build_slab(d0, half, xs, tail, v, cp):
    lane = lax.broadcasted_iota(jnp.int32, (16, LANE), 1)
    last = xs.shape[1] // LANE
    for g in range(cp // 16):
        rows = slice(16 * g, 16 * g + 16)

        def tile(t):
            return tail[rows, :] if t == last else xs[rows, LANE * t : LANE * t + LANE]

        for j in range(18):
            for kw in range(3):
                part = []
                for s1 in range(2):
                    p = (d0 + half * s1) * PW * PW + PW * j + kw
                    part.append(pltpu.roll(pair(tile, p, lane), (64 * s1 - p) % LANE, 1))
                r0 = (d0 * 3 + kw) * cp + 16 * g
                v[r0 : r0 + 16, LANE * j : LANE * j + LANE] = jnp.where(lane < 64, part[0], part[1])


def conv_part(d, half, taps, cp, qs, cot, v, outs):
    vox = HW * HW
    for c in range(2):
        lhs = []
        for q in qs[c]:
            for i in range(taps):
                t = jnp.minimum(q * taps + i, TAPS - 1)
                kd, kh, kw = t // 9, t // 3 % 3, t % 3
                r0 = pl.multiple_of(((d + kd) * 3 + kw) * cp, 16)
                lhs.append(v[pl.ds(r0, cp), pl.ds(pl.multiple_of(LANE * kh, LANE), 16 * LANE)])
        rhs = []
        for h in range(16):
            for s1 in range(2):
                for s0 in range(2):
                    r0 = (d + half * s1) * vox + (h + 16 * s0) * HW
                    rhs.append(cot[r0 : r0 + HW, 256 * c : 256 * c + 256])
        part = jnp.dot(jnp.concatenate(lhs, 0), jnp.concatenate(rhs, 0), preferred_element_type=F32)
        if d == 0:
            outs[c][...] = part
        else:
            outs[c][...] += part


def conv_kernel(depth, cp, taps, chunks, x_hbm, cot_hbm, *refs):
    outs = refs[:2]
    cot, v, xs, tail, xsem, csem = refs[2:]
    half = depth // 2
    ln = xs.shape[1]
    vox = HW * HW
    xcopy = pltpu.make_async_copy(x_hbm, xs, xsem)
    xcopy.start()
    copies = []
    for i in range(depth):
        rows = pl.ds(i * vox, vox)
        copies.append(pltpu.make_async_copy(cot_hbm.at[rows], cot.at[rows], csem.at[i]))
    for d in range(half):
        for s1 in range(2):
            copies[d + half * s1].start()
    xcopy.wait()
    n = ln // LANE * LANE
    if n < ln:
        tail[:, : ln - n] = xs[:, n:]
    for d0 in range(half + 2):
        build_slab(d0, half, xs, tail, v, cp)
    qs = chunks()
    for d in range(half):
        for s1 in range(2):
            copies[d + half * s1].wait()
        conv_part(d, half, taps, cp, qs, cot, v, outs)


def conv(x, cot, chunks, slots, taps):
    cp, ln = x.shape
    depth = cot.shape[0] // (HW * HW)
    return pl.pallas_call(
        functools.partial(conv_kernel, depth, cp, taps, chunks),
        out_shape=[pltpu.VMEM((slots * taps * cp, 256), F32)] * 2
        + [pltpu.VMEM(cot.shape, BF16), pltpu.VMEM((3 * (depth // 2 + 2) * cp, 18 * LANE), BF16)],
        in_specs=[HBM, HBM],
        out_specs=[VMEM] * 4,
        scratch_shapes=[
            pltpu.VMEM((cp, ln), BF16),
            pltpu.VMEM((cp, LANE), BF16),
            pltpu.SemaphoreType.DMA,
            pltpu.SemaphoreType.DMA((depth,)),
        ],
        compiler_params=params(),
        name="conv_first",
    )(x, cot)


def more_kernel(depth, cp, taps, chunks, cot, v, *outs):
    qs = chunks()
    for d in range(depth // 2):
        conv_part(d, depth // 2, taps, cp, qs, cot, v, outs)


def conv_more(cot, v, chunks, slots, taps, cp):
    depth = cot.shape[0] // (HW * HW)
    return pl.pallas_call(
        functools.partial(more_kernel, depth, cp, taps, chunks),
        out_shape=[pltpu.VMEM((slots * taps * cp, 256), F32)] * 2,
        in_specs=[VMEM] * 2,
        out_specs=[VMEM] * 2,
        compiler_params=params(),
        name="conv_more",
    )(near(cot), near(v))


def own_kernel(taps, cp, m_ref, o_ref):
    chans = m_ref.shape[0] // TAPS
    for i in range(taps):
        t = lax.axis_index("dp") * taps + i
        rows = m_ref[pl.ds(jnp.minimum(t, TAPS - 1), chans, stride=TAPS), :]
        o_ref[cp * i : cp * i + chans, :] = jnp.where(t < TAPS, rows, 0.0)
        if cp > chans:
            o_ref[cp * i + chans : cp * i + cp, :] = jnp.zeros((cp - chans, LANE), F32)


def own_momentum(momentum, taps, cp):
    return pl.pallas_call(
        functools.partial(own_kernel, taps, cp),
        out_shape=jax.ShapeDtypeStruct((taps * cp, momentum.shape[1]), F32),
        grid=(momentum.shape[1] // LANE,),
        in_specs=[column(momentum.shape[0])],
        out_specs=column(taps * cp),
        compiler_params=params(),
        name="own_momentum",
    )(momentum)


def split(x):
    hi = x.astype(BF16)
    return hi, (x - hi.astype(F32)).astype(BF16)


def dot_t(a, b):
    return lax.dot_general(a, b, (((0,), (0,)), ((), ())), preferred_element_type=F32)


def update(m, grad, taps, cp):
    tap = lax.axis_index("dp") * taps + lax.broadcasted_iota(jnp.int32, (taps * cp, 1), 0) // cp
    return jnp.where(tap < TAPS, 0.95 * m + grad, 0.0)


def update_kernel(taps, cp, m_ref, *refs):
    parts, outs = refs[:-2], refs[-2:]
    for c in range(2):
        grad = parts[c][...]
        for n in range(2 + c, len(parts), 2):
            grad = grad + parts[n][...]
        outs[c][...] = update(m_ref[:, 256 * c : 256 * c + 256], grad, taps, cp)


def momentum_update(own, parts, taps, cp):
    return pl.pallas_call(
        functools.partial(update_kernel, taps, cp),
        out_shape=[pltpu.VMEM((taps * cp, 256), F32)] * 2,
        in_specs=[VMEM] * (1 + len(parts)),
        out_specs=[VMEM] * 2,
        compiler_params=params(),
        name="momentum_update",
    )(near(own), *map(near, parts))


def upper_gram(m):
    hi, lo = split(m)
    out = []
    for i in range(4):
        a, b = slice(128 * i, 128 * i + 128), slice(128 * i, 512)
        out.append(dot_t(hi[:, a], hi[:, b]) + (dot_t(hi[:, a], lo[:, b]) + dot_t(lo[:, a], hi[:, b])))
    return out


def gram_kernel(ma, mb, keep, send):
    dp, core = lax.axis_index("dp"), lax.axis_index("shard") % 2
    gram = upper_gram(jnp.concatenate([ma[...], mb[...]], 1))
    for half in range(2):
        for n, (i, j) in enumerate(BLOCKS[half]):
            block = gram[i][:, 128 * (j - i) : 128 * (j - i) + 128]
            for r in range(4):
                piece = block[32 * r : 32 * r + 32]

                @pl.when(core == half)
                def _():
                    keep[r ^ dp, n] = piece

                @pl.when(core != half)
                def _():
                    send[r ^ dp, n] = piece


def own_gram(ma, mb):
    return pl.pallas_call(
        gram_kernel,
        out_shape=[pltpu.VMEM((4, 5, 32, 128), F32)] * 2,
        in_specs=[VMEM] * 2,
        out_specs=[VMEM] * 2,
        compiler_params=params(),
        name="own_gram",
    )(near(ma), near(mb))


def any_gram_kernel(ma, mb, g_ref):
    for i, rows in enumerate(upper_gram(jnp.concatenate([ma[...], mb[...]], 1))):
        g_ref[128 * i : 128 * i + 128, :] = jnp.zeros((128, 512), F32)
        g_ref[128 * i : 128 * i + 128, 128 * i :] = rows


def any_gram(ma, mb):
    return pl.pallas_call(
        any_gram_kernel,
        out_shape=jax.ShapeDtypeStruct((512, 512), F32),
        in_specs=[VMEM] * 2,
        out_specs=VMEM,
        compiler_params=params(),
        name="own_gram",
    )(near(ma), near(mb))


def order_kernel(taps, cp, chans, known, *refs):
    parts, (out, hi, lo, cols, sem) = refs[:-5], refs[-5:]
    copies = []
    for c in range(4):
        for r in range(len(parts) // 2):
            ref = parts[2 * r + c // 2]
            for i in range(ref.shape[0] // cp):
                t = (lax.axis_index("dp") ^ r) * taps + i if known else i
                if not known and i >= TAPS:
                    continue
                rows = ref[cp * i : cp * i + chans, LANE * (c % 2) : LANE * (c % 2) + LANE]

                @pl.when(t < TAPS)
                def _():
                    cols.at[c][pl.ds(t, chans, stride=TAPS), :] = rows

        copies.append(pltpu.make_async_copy(cols.at[c], out.at[:, pl.ds(LANE * c, LANE)], sem.at[c]))
        copies[c].start()
        hi[:, LANE * c : LANE * c + LANE], lo[:, LANE * c : LANE * c + LANE] = split(cols[c])
    for copy in copies:
        copy.wait()


def order(parts, taps, cp, chans, known):
    rows = chans * TAPS
    return pl.pallas_call(
        functools.partial(order_kernel, taps, cp, chans, known),
        out_shape=[jax.ShapeDtypeStruct((rows, 512), F32)] + [pltpu.VMEM((rows, 512), BF16)] * 2,
        in_specs=[VMEM] * len(parts),
        out_specs=[HBM, VMEM, VMEM],
        scratch_shapes=[pltpu.VMEM((4, rows, LANE), F32), pltpu.SemaphoreType.DMA((4,))],
        compiler_params=params(),
        name="weight_order",
    )(*map(near, parts))


def mm(a, b):
    ah, al = a
    bh, bl = b
    d = functools.partial(jnp.dot, preferred_element_type=F32)
    return d(ah, bh) + (d(ah, bl) + d(al, bh))


def row_cuts(rows):
    cuts = [min(rows, -(-rows * k // 24) * 8) for k in range(4)]
    return [(a, b) for a, b in zip(cuts, cuts[1:]) if b > a]


def apply_kernel(hi, lo, *refs):
    parts, (out, g_ref, acc, sem) = refs[:-4], refs[-4:]
    if len(parts) == 1:
        g_ref[...] = parts[0][...]
    else:
        dp, core = lax.axis_index("dp"), lax.axis_index("shard") % 2
        for n, part in enumerate(parts):
            which, r = divmod(n, 4)
            for half in range(2):

                @pl.when(core ^ which == half)
                def _():
                    for k, (i, j) in enumerate(BLOCKS[half]):
                        rows = pl.ds(pl.multiple_of(128 * i + 32 * (dp ^ r), 32), 32)
                        g_ref[rows, 128 * j : 128 * j + 128] = part[k]

    for i in range(4):
        for j in range(i + 1, 4):
            g_ref[128 * j : 128 * j + 128, 128 * i : 128 * i + 128] = g_ref[
                128 * i : 128 * i + 128, 128 * j : 128 * j + 128
            ].T
    gram = g_ref[...]
    n = gram.shape[0]
    diag = lax.broadcasted_iota(jnp.int32, (n, n), 0) == lax.broadcasted_iota(jnp.int32, (n, n), 1)
    trace = jnp.sum(jnp.where(diag, gram, 0.0), keepdims=True)
    scale = 1.0 / (jnp.sqrt(trace) + 1e-07)
    g = gram * scale * scale
    gs = split(g)
    p1 = jnp.where(diag, A1, 0.0) + B1 * g + C1 * mm(gs, gs)
    p1s = split(p1)
    g2 = mm(split(mm(gs, p1s)), p1s)
    g2s = split(g2)
    p2 = jnp.where(diag, A1, 0.0) + B1 * g2 + C1 * mm(g2s, g2s)
    qs = split(mm(p1s, split(p2)) * (scale * jnp.sqrt(F32(ROWS))))
    copies = []
    for k, (a, b) in enumerate(row_cuts(hi.shape[0])):
        acc[a:b, :] = mm((hi[a:b, :], lo[a:b, :]), qs)
        copies.append(pltpu.make_async_copy(acc.at[pl.ds(a, b - a)], out.at[pl.ds(a, b - a)], sem.at[k]))
        copies[k].start()
    for copy in copies:
        copy.wait()


def apply(hi, lo, parts):
    return pl.pallas_call(
        apply_kernel,
        out_shape=jax.ShapeDtypeStruct(hi.shape, F32),
        in_specs=[VMEM] * (2 + len(parts)),
        out_specs=HBM,
        scratch_shapes=[pltpu.VMEM((512, 512), F32), pltpu.VMEM(hi.shape, F32), pltpu.SemaphoreType.DMA((3,))],
        compiler_params=params(),
        name="newton_schulz",
    )(near(hi), near(lo), *map(near, parts))


def swap(x, axis, size, bit):
    return lax.ppermute(x, axis, [(i, i ^ bit) for i in range(size)])


def over_x(x):
    return swap(x, "dp", 4, 1)


def over_y(x):
    return swap(x, "dp", 4, 2)


def over_core(x):
    return swap(x, "shard", 8, 1)


def chunk_pair(a, b):
    def chunks():
        dp = lax.axis_index("dp")
        return [dp ^ a], [dp ^ b]

    return chunks


def body_4x8(layer_input, cotangent, momentum):
    chans = momentum.shape[0] // TAPS
    cp = layer_input.shape[0]
    taps = 7
    a3, b3, cot, v = conv(layer_input, cotangent, chunk_pair(3, 3), 1, taps)
    a3, b3 = over_x(a3), over_y(b3)
    a1, b1 = conv_more(cot, v, chunk_pair(1, 2), 1, taps, cp)
    a1, b1 = over_x(a1), over_y(b1)
    a2, b2 = conv_more(cot, v, chunk_pair(2, 1), 1, taps, cp)
    a2, b2 = over_y(a2 + a3), over_x(b2 + b3)
    a0, b0 = conv_more(cot, v, chunk_pair(0, 0), 1, taps, cp)
    own = own_momentum(momentum, taps, cp)
    ma, mb = momentum_update(own, (a0, b0, a1, b1, a2, b2), taps, cp)
    max_, mby = over_x(ma), over_y(mb)
    keep, send = own_gram(ma, mb)
    g = keep + over_core(send)
    g = g[0] + over_x(g[1]) + over_y(g[2]) + swap(g[3], "dp", 4, 3)
    ma_, mb_, max_, mby, g = lax.optimization_barrier((ma, mb, max_, mby, g))
    may, mbx, mad, mbd = over_y(ma_), over_x(mb_), over_y(max_), over_x(mby)
    g = g + swap(g, "shard", 8, 2) + swap(g, "shard", 8, 4) + swap(g, "shard", 8, 6)
    g = [g] + [swap(g, "dp", 4, r) for r in (1, 2, 3)]
    g = g + [over_core(x) for x in g]
    momentum_new, hi, lo = order((ma, mb, max_, mbx, may, mby, mad, mbd), taps, cp, chans, True)
    return momentum_new, apply(hi, lo, g)


def body_any(n_dp, layer_input, cotangent, momentum):
    chans = layer_input.shape[0]
    cp = -(-chans // 16) * 16
    taps = -(-TAPS // n_dp)
    x = jnp.pad(layer_input, ((0, cp - chans), (0, 0)))
    part = conv(x, cotangent, lambda: [list(range(n_dp))] * 2, n_dp, taps)[:2]
    grad = [lax.psum_scatter(p, "dp", scatter_dimension=0, tiled=True) for p in part]
    ma, mb = momentum_update(own_momentum(momentum, taps, cp), grad, taps, cp)
    gram = lax.psum(any_gram(ma, mb), ("dp", "shard"))
    full = [lax.all_gather(m, "dp", axis=0, tiled=True) for m in (ma, mb)]
    momentum_new, hi, lo = order(full, taps, cp, chans, False)
    return momentum_new, apply(hi, lo, [gram])


def solution(mesh):
    n_dp = mesh.shape["dp"]
    known = (n_dp, mesh.shape["shard"]) == (4, 8)
    return jax.shard_map(
        body_4x8 if known else functools.partial(body_any, n_dp),
        mesh=mesh,
        in_specs=(P("shard", "dp"), P("dp", None), P("shard", None)),
        out_specs=(P("shard", None), P("shard", None)),
        check_vma=False,
    )
```

```python
import functools

import jax
import jax.numpy as jnp
from jax import lax
from jax.experimental import pallas as pl
from jax.experimental.pallas import tpu as pltpu
from jax.sharding import PartitionSpec as P

HW = 32
ROWS = 10368
PW = HW + 2
LANE = 128
TAPS = 27
A1, B1, C1 = 3.4445, -4.775, 2.0315
F32 = jnp.float32
BF16 = jnp.bfloat16
VMEM = pl.BlockSpec(memory_space=pltpu.VMEM)
HBM = pl.BlockSpec(memory_space=pltpu.HBM)
BLOCKS = (((0, 0), (0, 1), (0, 2), (0, 3), (1, 1)), ((1, 2), (1, 3), (2, 2), (2, 3), (3, 3)))


def column(rows):
    return pl.BlockSpec((rows, LANE), lambda c: (0, c))


def params(mib=24):
    return pltpu.CompilerParams(vmem_limit_bytes=mib << 20)


def near(x):
    return pltpu.with_memory_space_constraint(x, pltpu.VMEM)


def far(x):
    return pltpu.with_memory_space_constraint(x, pltpu.HBM)


def pair(tile, p, lane):
    t, c = divmod(p, LANE)
    if c + 64 <= LANE:
        return jnp.where(lane < c + 32, tile(t), tile(t + 4))
    if c + 32 <= LANE:
        far = jnp.where(lane < c, tile(t + 5), tile(t))
        if c + 32 == LANE:
            return far
        return jnp.where(lane < c + 32, far, tile(t + 4))
    near = jnp.where(lane < c + 32 - LANE, tile(t + 1), tile(t + 5))
    return jnp.where(lane < c, near, tile(t))


def build_slab(d0, half, xs, tail, v, cp):
    lane = lax.broadcasted_iota(jnp.int32, (16, LANE), 1)
    last = xs.shape[1] // LANE
    for g in range(cp // 16):
        rows = slice(16 * g, 16 * g + 16)

        def tile(t):
            return tail[rows, :] if t == last else xs[rows, LANE * t : LANE * t + LANE]

        for j in range(18):
            for kw in range(3):
                part = []
                for s1 in range(2):
                    p = (d0 + half * s1) * PW * PW + PW * j + kw
                    part.append(pltpu.roll(pair(tile, p, lane), (64 * s1 - p) % LANE, 1))
                r0 = (d0 * 3 + kw) * cp + 16 * g
                v[r0 : r0 + 16, LANE * j : LANE * j + LANE] = jnp.where(lane < 64, part[0], part[1])


def conv_part(d, half, taps, cp, qs, cot, v, outs):
    vox = HW * HW
    for c in range(2):
        lhs = []
        for q in qs[c]:
            for i in range(taps):
                t = jnp.minimum(q * taps + i, TAPS - 1)
                kd, kh, kw = t // 9, t // 3 % 3, t % 3
                r0 = pl.multiple_of(((d + kd) * 3 + kw) * cp, 16)
                lhs.append(v[pl.ds(r0, cp), pl.ds(pl.multiple_of(LANE * kh, LANE), 16 * LANE)])
        rhs = []
        for h in range(16):
            for s1 in range(2):
                for s0 in range(2):
                    r0 = (d + half * s1) * vox + (h + 16 * s0) * HW
                    rhs.append(cot[r0 : r0 + HW, 256 * c : 256 * c + 256])
        part = jnp.dot(jnp.concatenate(lhs, 0), jnp.concatenate(rhs, 0), preferred_element_type=F32)
        if d == 0:
            outs[c][...] = part
        else:
            outs[c][...] += part


def conv_kernel(depth, cp, taps, chunks, x_hbm, cot_hbm, *refs):
    outs = refs[:2]
    cot, v, xs, tail, xsem, csem = refs[2:]
    half = depth // 2
    ln = xs.shape[1]
    vox = HW * HW
    xcopy = pltpu.make_async_copy(x_hbm, xs, xsem)
    xcopy.start()
    copies = []
    for i in range(depth):
        rows = pl.ds(i * vox, vox)
        copies.append(pltpu.make_async_copy(cot_hbm.at[rows], cot.at[rows], csem.at[i]))
    for d in range(half):
        for s1 in range(2):
            copies[d + half * s1].start()
    xcopy.wait()
    n = ln // LANE * LANE
    if n < ln:
        tail[:, : ln - n] = xs[:, n:]
    for d0 in range(half + 2):
        build_slab(d0, half, xs, tail, v, cp)
    qs = chunks()
    for d in range(half):
        for s1 in range(2):
            copies[d + half * s1].wait()
        conv_part(d, half, taps, cp, qs, cot, v, outs)


def conv(x, cot, chunks, slots, taps):
    cp, ln = x.shape
    depth = cot.shape[0] // (HW * HW)
    return pl.pallas_call(
        functools.partial(conv_kernel, depth, cp, taps, chunks),
        out_shape=[pltpu.VMEM((slots * taps * cp, 256), F32)] * 2
        + [pltpu.VMEM(cot.shape, BF16), pltpu.VMEM((3 * (depth // 2 + 2) * cp, 18 * LANE), BF16)],
        in_specs=[HBM, HBM],
        out_specs=[VMEM] * 4,
        scratch_shapes=[
            pltpu.VMEM((cp, ln), BF16),
            pltpu.VMEM((cp, LANE), BF16),
            pltpu.SemaphoreType.DMA,
            pltpu.SemaphoreType.DMA((depth,)),
        ],
        compiler_params=params(),
        name="conv_first",
    )(far(x), far(cot))


def more_kernel(depth, cp, taps, chunks, cot, v, *outs):
    qs = chunks()
    for d in range(depth // 2):
        conv_part(d, depth // 2, taps, cp, qs, cot, v, outs)


def conv_more(cot, v, chunks, slots, taps, cp):
    depth = cot.shape[0] // (HW * HW)
    return pl.pallas_call(
        functools.partial(more_kernel, depth, cp, taps, chunks),
        out_shape=[pltpu.VMEM((slots * taps * cp, 256), F32)] * 2,
        in_specs=[VMEM] * 2,
        out_specs=[VMEM] * 2,
        compiler_params=params(),
        name="conv_more",
    )(near(cot), near(v))


def own_kernel(taps, cp, m_ref, o_ref):
    chans = m_ref.shape[0] // TAPS
    for i in range(taps):
        t = lax.axis_index("dp") * taps + i
        rows = m_ref[pl.ds(jnp.minimum(t, TAPS - 1), chans, stride=TAPS), :]
        o_ref[cp * i : cp * i + chans, :] = jnp.where(t < TAPS, rows, 0.0)
        if cp > chans:
            o_ref[cp * i + chans : cp * i + cp, :] = jnp.zeros((cp - chans, LANE), F32)


def own_momentum(momentum, taps, cp):
    return pl.pallas_call(
        functools.partial(own_kernel, taps, cp),
        out_shape=jax.ShapeDtypeStruct((taps * cp, momentum.shape[1]), F32),
        grid=(momentum.shape[1] // LANE,),
        in_specs=[column(momentum.shape[0])],
        out_specs=column(taps * cp),
        compiler_params=params(),
        name="own_momentum",
    )(momentum)


def split(x):
    hi = x.astype(BF16)
    return hi, (x - hi.astype(F32)).astype(BF16)


def dot_t(a, b):
    return lax.dot_general(a, b, (((0,), (0,)), ((), ())), preferred_element_type=F32)


def update(m, grad, taps, cp):
    tap = lax.axis_index("dp") * taps + lax.broadcasted_iota(jnp.int32, (taps * cp, 1), 0) // cp
    return jnp.where(tap < TAPS, 0.95 * m + grad, 0.0)


def update_kernel(taps, cp, m_ref, *refs):
    parts, out = refs[:-1], refs[-1]
    rows = taps * cp
    for c in range(2):
        grad = parts[c][...]
        for n in range(2 + c, len(parts), 2):
            grad = grad + parts[n][...]
        out[rows * c : rows * c + rows, :] = update(m_ref[:, 256 * c : 256 * c + 256], grad, taps, cp)


def momentum_update(own, parts, taps, cp):
    return pl.pallas_call(
        functools.partial(update_kernel, taps, cp),
        out_shape=pltpu.VMEM((2 * taps * cp, 256), F32),
        in_specs=[VMEM] * (1 + len(parts)),
        out_specs=VMEM,
        compiler_params=params(),
        name="momentum_update",
    )(near(own), *map(near, parts))


def upper_gram(m):
    hi, lo = split(m)
    out = []
    for i in range(4):
        a, b = slice(128 * i, 128 * i + 128), slice(128 * i, 512)
        out.append(dot_t(hi[:, a], hi[:, b]) + (dot_t(hi[:, a], lo[:, b]) + dot_t(lo[:, a], hi[:, b])))
    return out


def gram_kernel(m, keep, send):
    z, core = lax.axis_index("shard") // 2, lax.axis_index("shard") % 2
    rows = m.shape[0] // 2
    gram = upper_gram(jnp.concatenate([m[:rows], m[rows:]], 1))
    for half in range(2):
        for n, (i, j) in enumerate(BLOCKS[half]):
            block = gram[i][:, 128 * (j - i) : 128 * (j - i) + 128]
            for r in range(4):
                piece = block[32 * r : 32 * r + 32]

                @pl.when(core == half)
                def _():
                    keep[r ^ z, n] = piece

                @pl.when(core != half)
                def _():
                    send[r ^ z, n] = piece


def own_gram(m):
    return pl.pallas_call(
        gram_kernel,
        out_shape=[pltpu.VMEM((4, 5, 32, 128), F32)] * 2,
        in_specs=[VMEM],
        out_specs=[VMEM] * 2,
        compiler_params=params(),
        name="own_gram",
    )(near(m))


def any_gram_kernel(m, g_ref):
    half = m.shape[0] // 2
    for i, rows in enumerate(upper_gram(jnp.concatenate([m[:half], m[half:]], 1))):
        g_ref[128 * i : 128 * i + 128, :] = jnp.zeros((128, 512), F32)
        g_ref[128 * i : 128 * i + 128, 128 * i :] = rows


def any_gram(m):
    return pl.pallas_call(
        any_gram_kernel,
        out_shape=jax.ShapeDtypeStruct((512, 512), F32),
        in_specs=[VMEM],
        out_specs=VMEM,
        compiler_params=params(),
        name="own_gram",
    )(near(m))


def order_kernel(taps, cp, chans, known, stacked, *refs):
    parts, (out, hi, lo, cols, sem) = refs[:-5], refs[-5:]
    copies = []
    for c in range(4):
        for r in range(len(parts) // 2):
            ref = parts[2 * r + c // 2]
            base = ref.shape[0] // 2 * (c // 2) if stacked[r] else 0
            for i in range(ref.shape[0] // cp // (2 if stacked[r] else 1)):
                t = (lax.axis_index("dp") ^ r) * taps + i if known else i
                if not known and i >= TAPS:
                    continue
                rows = ref[base + cp * i : base + cp * i + chans, LANE * (c % 2) : LANE * (c % 2) + LANE]

                @pl.when(t < TAPS)
                def _():
                    cols.at[c][pl.ds(t, chans, stride=TAPS), :] = rows

        copies.append(pltpu.make_async_copy(cols.at[c], out.at[:, pl.ds(LANE * c, LANE)], sem.at[c]))
        copies[c].start()
        hi[:, LANE * c : LANE * c + LANE], lo[:, LANE * c : LANE * c + LANE] = split(cols[c])
    for copy in copies:
        copy.wait()


def order(parts, taps, cp, chans, known):
    rows = chans * TAPS
    stacked = [a is b for a, b in zip(parts[::2], parts[1::2])]
    return pl.pallas_call(
        functools.partial(order_kernel, taps, cp, chans, known, stacked),
        out_shape=[jax.ShapeDtypeStruct((rows, 512), F32)] + [pltpu.VMEM((rows, 512), BF16)] * 2,
        in_specs=[VMEM] * len(parts),
        out_specs=[HBM, VMEM, VMEM],
        scratch_shapes=[pltpu.VMEM((4, rows, LANE), F32), pltpu.SemaphoreType.DMA((4,))],
        compiler_params=params(),
        name="weight_order",
    )(*map(near, parts))


def mm(a, b):
    ah, al = a
    bh, bl = b
    d = functools.partial(jnp.dot, preferred_element_type=F32)
    return d(ah, bh) + (d(ah, bl) + d(al, bh))


def row_cuts(rows):
    cuts = [min(rows, -(-rows * k // 24) * 8) for k in range(4)]
    return [(a, b) for a, b in zip(cuts, cuts[1:]) if b > a]


def apply_kernel(hi, lo, *refs):
    parts, (out, g_ref, acc, sem) = refs[:-4], refs[-4:]
    if len(parts) == 1:
        g_ref[...] = parts[0][...]
    else:
        z, core = lax.axis_index("shard") // 2, lax.axis_index("shard") % 2
        for n, part in enumerate(parts):
            which, r = divmod(n, 4)
            for half in range(2):

                @pl.when(core ^ which == half)
                def _():
                    for k, (i, j) in enumerate(BLOCKS[half]):
                        rows = pl.ds(pl.multiple_of(128 * i + 32 * (z ^ r), 32), 32)
                        g_ref[rows, 128 * j : 128 * j + 128] = part[k]

    for i in range(4):
        for j in range(i + 1, 4):
            g_ref[128 * j : 128 * j + 128, 128 * i : 128 * i + 128] = g_ref[
                128 * i : 128 * i + 128, 128 * j : 128 * j + 128
            ].T
    gram = g_ref[...]
    n = gram.shape[0]
    diag = lax.broadcasted_iota(jnp.int32, (n, n), 0) == lax.broadcasted_iota(jnp.int32, (n, n), 1)
    trace = jnp.sum(jnp.where(diag, gram, 0.0), keepdims=True)
    scale = 1.0 / (jnp.sqrt(trace) + 1e-07)
    g = gram * scale * scale
    gs = split(g)
    p1 = jnp.where(diag, A1, 0.0) + B1 * g + C1 * mm(gs, gs)
    p1s = split(p1)
    g2 = mm(split(mm(gs, p1s)), p1s)
    g2s = split(g2)
    p2 = jnp.where(diag, A1, 0.0) + B1 * g2 + C1 * mm(g2s, g2s)
    qs = split(mm(p1s, split(p2)) * (scale * jnp.sqrt(F32(ROWS))))
    copies = []
    for k, (a, b) in enumerate(row_cuts(hi.shape[0])):
        acc[a:b, :] = mm((hi[a:b, :], lo[a:b, :]), qs)
        copies.append(pltpu.make_async_copy(acc.at[pl.ds(a, b - a)], out.at[pl.ds(a, b - a)], sem.at[k]))
        copies[k].start()
    for copy in copies:
        copy.wait()


def apply(hi, lo, parts):
    return pl.pallas_call(
        apply_kernel,
        out_shape=jax.ShapeDtypeStruct(hi.shape, F32),
        in_specs=[VMEM] * (2 + len(parts)),
        out_specs=HBM,
        scratch_shapes=[pltpu.VMEM((512, 512), F32), pltpu.VMEM(hi.shape, F32), pltpu.SemaphoreType.DMA((3,))],
        compiler_params=params(),
        name="newton_schulz",
    )(near(hi), near(lo), *map(near, parts))


def swap(x, axis, size, bit):
    return lax.ppermute(x, axis, [(i, i ^ bit) for i in range(size)])


def over_x(x):
    return swap(x, "dp", 4, 1)


def over_y(x):
    return swap(x, "dp", 4, 2)


def over_core(x):
    return swap(x, "shard", 8, 1)


def over_z(x, r):
    return swap(x, "shard", 8, 2 * r)


def chunk_pair(a, b):
    def chunks():
        dp = lax.axis_index("dp")
        return [dp ^ a], [dp ^ b]

    return chunks


def body_4x8(layer_input, cotangent, momentum):
    chans = momentum.shape[0] // TAPS
    cp = layer_input.shape[0]
    taps = 7
    a3, b3, cot, v = conv(layer_input, cotangent, chunk_pair(3, 3), 1, taps)
    a3, b3 = over_x(a3), over_y(b3)
    a1, b1 = conv_more(cot, v, chunk_pair(1, 2), 1, taps, cp)
    a1, b1 = over_x(a1), over_y(b1)
    a2, b2 = conv_more(cot, v, chunk_pair(2, 1), 1, taps, cp)
    a2, b2 = over_y(a2 + a3), over_x(b2 + b3)
    a0, b0 = conv_more(cot, v, chunk_pair(0, 0), 1, taps, cp)
    own = own_momentum(momentum, taps, cp)
    m = momentum_update(own, (a0, b0, a1, b1, a2, b2), taps, cp)
    mx, my = over_x(m), over_y(m)
    keep, send = own_gram(m)
    g = keep + over_core(send)
    g = g[0] + over_z(g[1], 1) + over_z(g[2], 2) + over_z(g[3], 3)
    g = (g + over_x(g)) + (over_y(g) + swap(g, "dp", 4, 3))
    g = [g] + [over_z(g, r) for r in (1, 2, 3)]
    g = g + [over_core(x) for x in g]
    rows = taps * cp
    ad, bd = over_y(mx[:rows]), over_x(my[rows:])
    momentum_new, hi, lo = order((m, m, mx, mx, my, my, ad, bd), taps, cp, chans, True)
    return momentum_new, apply(hi, lo, g)


def body_any(n_dp, layer_input, cotangent, momentum):
    chans = layer_input.shape[0]
    cp = -(-chans // 16) * 16
    taps = -(-TAPS // n_dp)
    x = jnp.pad(layer_input, ((0, cp - chans), (0, 0)))
    part = conv(x, cotangent, lambda: [list(range(n_dp))] * 2, n_dp, taps)[:2]
    grad = [lax.psum_scatter(p, "dp", scatter_dimension=0, tiled=True) for p in part]
    m = momentum_update(own_momentum(momentum, taps, cp), grad, taps, cp)
    gram = lax.psum(any_gram(m), ("dp", "shard"))
    rows = taps * cp
    full = [lax.all_gather(half, "dp", axis=0, tiled=True) for half in (m[:rows], m[rows:])]
    momentum_new, hi, lo = order(full, taps, cp, chans, False)
    return momentum_new, apply(hi, lo, [gram])


def solution(mesh):
    n_dp = mesh.shape["dp"]
    known = (n_dp, mesh.shape["shard"]) == (4, 8)
    return jax.shard_map(
        body_4x8 if known else functools.partial(body_any, n_dp),
        mesh=mesh,
        in_specs=(P("shard", "dp"), P("dp", None), P("shard", None)),
        out_specs=(P("shard", None), P("shard", None)),
        check_vma=False,
    )
```

```python
import functools

import jax
import jax.numpy as jnp
from jax import lax
from jax.experimental import pallas as pl
from jax.experimental.pallas import tpu as pltpu
from jax.sharding import PartitionSpec as P

HW = 32
ROWS = 10368
PW = HW + 2
LANE = 128
TAPS = 27
A1, B1, C1 = 3.4445, -4.775, 2.0315
F32 = jnp.float32
BF16 = jnp.bfloat16
VMEM = pl.BlockSpec(memory_space=pltpu.VMEM)
HBM = pl.BlockSpec(memory_space=pltpu.HBM)
BLOCKS = (((0, 1), (0, 2), (0, 3)), ((1, 2), (1, 3), (2, 3)))
PIECE = (136, 128)


def column(rows):
    return pl.BlockSpec((rows, LANE), lambda c: (0, c))


def params(mib=24):
    return pltpu.CompilerParams(vmem_limit_bytes=mib << 20)


def near(x):
    return pltpu.with_memory_space_constraint(x, pltpu.VMEM)


def far(x):
    return pltpu.with_memory_space_constraint(x, pltpu.HBM)


def pair(tile, p, lane):
    t, c = divmod(p, LANE)
    if c + 64 <= LANE:
        return jnp.where(lane < c + 32, tile(t), tile(t + 4))
    if c + 32 <= LANE:
        far = jnp.where(lane < c, tile(t + 5), tile(t))
        if c + 32 == LANE:
            return far
        return jnp.where(lane < c + 32, far, tile(t + 4))
    near = jnp.where(lane < c + 32 - LANE, tile(t + 1), tile(t + 5))
    return jnp.where(lane < c, near, tile(t))


def build_slab(d0, half, g, xs, tail, v, cp):
    lane = lax.broadcasted_iota(jnp.int32, (16, LANE), 1)
    last = xs.shape[1] // LANE
    rows = slice(16 * g, 16 * g + 16)

    def tile(t):
        return tail[rows, :] if t == last else xs[rows, LANE * t : LANE * t + LANE]

    for j in range(18):
        for kw in range(3):
            part = []
            for s1 in range(2):
                p = (d0 + half * s1) * PW * PW + PW * j + kw
                part.append(pltpu.roll(pair(tile, p, lane), (64 * s1 - p) % LANE, 1))
            r0 = (d0 * 3 + kw) * cp + 16 * g
            v[r0 : r0 + 16, LANE * j : LANE * j + LANE] = jnp.where(lane < 64, part[0], part[1])


def conv_part(d, half, taps, cp, qs, cot, v, outs):
    vox = HW * HW
    for c in range(2):
        lhs = []
        for q in qs[c]:
            for i in range(taps):
                t = jnp.minimum(q * taps + i, TAPS - 1)
                kd, kh, kw = t // 9, t // 3 % 3, t % 3
                r0 = pl.multiple_of(((d + kd) * 3 + kw) * cp, 16)
                lhs.append(v[pl.ds(r0, cp), pl.ds(pl.multiple_of(LANE * kh, LANE), 16 * LANE)])
        rhs = []
        for h in range(16):
            for s1 in range(2):
                for s0 in range(2):
                    r0 = (d + half * s1) * vox + (h + 16 * s0) * HW
                    rhs.append(cot[r0 : r0 + HW, 256 * c : 256 * c + 256])
        part = jnp.dot(jnp.concatenate(lhs, 0), jnp.concatenate(rhs, 0), preferred_element_type=F32)
        if d == 0:
            outs[c][...] = part
        else:
            outs[c][...] += part


def conv_kernel(depth, cp, taps, chunks, x_hbm, cot_hbm, *refs):
    outs = refs[:2]
    cot, v, xs, tail, xsem, csem = refs[2:]
    half = depth // 2
    ln = xs.shape[1]
    vox = HW * HW
    groups = [pl.ds(16 * g, 16) for g in range(cp // 16)]
    xcopies = [pltpu.make_async_copy(x_hbm.at[r], xs.at[r], xsem.at[g]) for g, r in enumerate(groups)]
    for copy in xcopies:
        copy.start()
    copies = []
    for i in range(depth):
        rows = pl.ds(i * vox, vox)
        copies.append(pltpu.make_async_copy(cot_hbm.at[rows], cot.at[rows], csem.at[i]))
    n = ln // LANE * LANE
    for g, copy in enumerate(xcopies):
        copy.wait()
        if g == 0:
            for d in range(half):
                for s1 in range(2):
                    copies[d + half * s1].start()
        if n < ln:
            tail[16 * g : 16 * g + 16, : ln - n] = xs[16 * g : 16 * g + 16, n:]
        for d0 in range(half + 2):
            build_slab(d0, half, g, xs, tail, v, cp)
    qs = chunks()
    for d in range(half):
        for s1 in range(2):
            copies[d + half * s1].wait()
        conv_part(d, half, taps, cp, qs, cot, v, outs)


def conv(x, cot, chunks, slots, taps):
    cp, ln = x.shape
    depth = cot.shape[0] // (HW * HW)
    return pl.pallas_call(
        functools.partial(conv_kernel, depth, cp, taps, chunks),
        out_shape=[pltpu.VMEM((slots * taps * cp, 256), F32)] * 2
        + [pltpu.VMEM(cot.shape, BF16), pltpu.VMEM((3 * (depth // 2 + 2) * cp, 18 * LANE), BF16)],
        in_specs=[HBM, HBM],
        out_specs=[VMEM] * 4,
        scratch_shapes=[
            pltpu.VMEM((cp, ln), BF16),
            pltpu.VMEM((cp, LANE), BF16),
            pltpu.SemaphoreType.DMA((cp // 16,)),
            pltpu.SemaphoreType.DMA((depth,)),
        ],
        compiler_params=params(),
        name="conv_first",
    )(far(x), far(cot))


def more_kernel(depth, cp, taps, chunks, cot, v, *outs):
    qs = chunks()
    for d in range(depth // 2):
        conv_part(d, depth // 2, taps, cp, qs, cot, v, outs)


def conv_more(cot, v, chunks, slots, taps, cp):
    depth = cot.shape[0] // (HW * HW)
    return pl.pallas_call(
        functools.partial(more_kernel, depth, cp, taps, chunks),
        out_shape=[pltpu.VMEM((slots * taps * cp, 256), F32)] * 2,
        in_specs=[VMEM] * 2,
        out_specs=[VMEM] * 2,
        compiler_params=params(),
        name="conv_more",
    )(near(cot), near(v))


def own_kernel(taps, cp, m_ref, o_ref):
    chans = m_ref.shape[0] // TAPS
    for i in range(taps):
        t = lax.axis_index("dp") * taps + i
        rows = m_ref[pl.ds(jnp.minimum(t, TAPS - 1), chans, stride=TAPS), :]
        o_ref[cp * i : cp * i + chans, :] = jnp.where(t < TAPS, rows, 0.0)
        if cp > chans:
            o_ref[cp * i + chans : cp * i + cp, :] = jnp.zeros((cp - chans, LANE), F32)


def own_momentum(momentum, taps, cp):
    return pl.pallas_call(
        functools.partial(own_kernel, taps, cp),
        out_shape=jax.ShapeDtypeStruct((taps * cp, momentum.shape[1]), F32),
        grid=(momentum.shape[1] // LANE,),
        in_specs=[column(momentum.shape[0])],
        out_specs=column(taps * cp),
        compiler_params=params(),
        name="own_momentum",
    )(momentum)


def split(x):
    hi = x.astype(BF16)
    return hi, (x - hi.astype(F32)).astype(BF16)


def dot_t(a, b):
    return lax.dot_general(a, b, (((0,), (0,)), ((), ())), preferred_element_type=F32)


def update(m, grad, taps, cp):
    tap = lax.axis_index("dp") * taps + lax.broadcasted_iota(jnp.int32, (taps * cp, 1), 0) // cp
    return jnp.where(tap < TAPS, 0.95 * m + grad, 0.0)


def update_kernel(taps, cp, m_ref, *refs):
    parts, out = refs[:-1], refs[-1]
    rows = taps * cp
    for c in range(2):
        grad = parts[c][...]
        for n in range(2 + c, len(parts), 2):
            grad = grad + parts[n][...]
        out[rows * c : rows * c + rows, :] = update(m_ref[:, 256 * c : 256 * c + 256], grad, taps, cp)


def momentum_update(own, parts, taps, cp):
    return pl.pallas_call(
        functools.partial(update_kernel, taps, cp),
        out_shape=pltpu.VMEM((2 * taps * cp, 256), F32),
        in_specs=[VMEM] * (1 + len(parts)),
        out_specs=VMEM,
        compiler_params=params(),
        name="momentum_update",
    )(near(own), *map(near, parts))


def upper_gram(m):
    hi, lo = split(m)
    out = []
    for i in range(4):
        a, b = slice(128 * i, 128 * i + 128), slice(128 * i, 512)
        out.append(dot_t(hi[:, a], hi[:, b]) + (dot_t(hi[:, a], lo[:, b]) + dot_t(lo[:, a], hi[:, b])))
    return out


def gram_kernel(m, keep, send):
    z, core = lax.axis_index("shard") // 2, lax.axis_index("shard") % 2
    rows = m.shape[0] // 2
    gram = upper_gram(jnp.concatenate([m[:rows], m[rows:]], 1))
    row = lax.broadcasted_iota(jnp.int32, (128, 128), 0)
    col = lax.broadcasted_iota(jnp.int32, (128, 128), 1)
    for half in range(2):
        blocks = [gram[i][:, 128 * (j - i) : 128 * (j - i) + 128] for i, j in BLOCKS[half]]
        even, odd = gram[2 * half][:, :128], gram[2 * half + 1][:, :128]
        blocks.append(jnp.where(row <= col, even, odd))
        diag = jnp.where(row == col, odd, 0.0)
        for r in range(4):
            cut = slice(32 * r, 32 * r + 32)
            last = jnp.sum(diag[cut], axis=0, keepdims=True)
            last = jnp.where(row[:8] == 0, jnp.broadcast_to(last, (8, 128)), 0.0)
            piece = jnp.concatenate([block[cut] for block in blocks] + [last], 0)

            @pl.when(core == half)
            def _():
                keep[r ^ z] = piece

            @pl.when(core != half)
            def _():
                send[r ^ z] = piece


def own_gram(m):
    return pl.pallas_call(
        gram_kernel,
        out_shape=[pltpu.VMEM((4,) + PIECE, F32)] * 2,
        in_specs=[VMEM],
        out_specs=[VMEM] * 2,
        compiler_params=params(),
        name="own_gram",
    )(near(m))


def any_gram_kernel(m, g_ref):
    half = m.shape[0] // 2
    for i, rows in enumerate(upper_gram(jnp.concatenate([m[:half], m[half:]], 1))):
        g_ref[128 * i : 128 * i + 128, :] = jnp.zeros((128, 512), F32)
        g_ref[128 * i : 128 * i + 128, 128 * i :] = rows


def any_gram(m):
    return pl.pallas_call(
        any_gram_kernel,
        out_shape=jax.ShapeDtypeStruct((512, 512), F32),
        in_specs=[VMEM],
        out_specs=VMEM,
        compiler_params=params(),
        name="own_gram",
    )(near(m))


def order_kernel(taps, cp, chans, known, stacked, *refs):
    parts, (out, hi, lo, cols, sem) = refs[:-5], refs[-5:]
    copies = []
    for c in range(4):
        for r in range(len(parts) // 2):
            ref = parts[2 * r + c // 2]
            base = ref.shape[0] // 2 * (c // 2) if stacked[r] else 0
            for i in range(ref.shape[0] // cp // (2 if stacked[r] else 1)):
                t = (lax.axis_index("dp") ^ r) * taps + i if known else i
                if not known and i >= TAPS:
                    continue
                rows = ref[base + cp * i : base + cp * i + chans, LANE * (c % 2) : LANE * (c % 2) + LANE]

                @pl.when(t < TAPS)
                def _():
                    cols.at[c][pl.ds(t, chans, stride=TAPS), :] = rows

        copies.append(pltpu.make_async_copy(cols.at[c], out.at[:, pl.ds(LANE * c, LANE)], sem.at[c]))
        copies[c].start()
        hi[:, LANE * c : LANE * c + LANE], lo[:, LANE * c : LANE * c + LANE] = split(cols[c])
    for copy in copies:
        copy.wait()


def order(parts, taps, cp, chans, known):
    rows = chans * TAPS
    stacked = [a is b for a, b in zip(parts[::2], parts[1::2])]
    return pl.pallas_call(
        functools.partial(order_kernel, taps, cp, chans, known, stacked),
        out_shape=[jax.ShapeDtypeStruct((rows, 512), F32)] + [pltpu.VMEM((rows, 512), BF16)] * 2,
        in_specs=[VMEM] * len(parts),
        out_specs=[HBM, VMEM, VMEM],
        scratch_shapes=[pltpu.VMEM((4, rows, LANE), F32), pltpu.SemaphoreType.DMA((4,))],
        compiler_params=params(),
        name="weight_order",
    )(*map(near, parts))


def mm(a, b):
    ah, al = a
    bh, bl = b
    d = functools.partial(jnp.dot, preferred_element_type=F32)
    return d(ah, bh) + (d(ah, bl) + d(al, bh))


def row_cuts(rows):
    cuts = [min(rows, -(-rows * k // 24) * 8) for k in range(4)]
    return [(a, b) for a, b in zip(cuts, cuts[1:]) if b > a]


def apply_kernel(hi, lo, *refs):
    parts, (out, g_ref, p_ref, d_ref, acc, sem) = refs[:-6], refs[-6:]
    if len(parts) == 1:
        g_ref[...] = parts[0][...]
    else:
        z, core = lax.axis_index("shard") // 2, lax.axis_index("shard") % 2
        for n, part in enumerate(parts):
            which, r = n // 4, 3 - n % 4
            q = z ^ r
            for half in range(2):

                @pl.when(core ^ which == half)
                def _():
                    for k, (i, j) in enumerate(BLOCKS[half]):
                        rows = pl.ds(pl.multiple_of(128 * i + 32 * q, 32), 32)
                        g_ref[rows, 128 * j : 128 * j + 128] = part[32 * k : 32 * k + 32]
                    p_ref[half, pl.ds(pl.multiple_of(32 * q, 32), 32), :] = part[96:128]
                    d_ref[half, 8 * r : 8 * r + 8, :] = part[128:136]

        row = lax.broadcasted_iota(jnp.int32, (128, 128), 0)
        col = lax.broadcasted_iota(jnp.int32, (128, 128), 1)
        for half in range(2):
            up = p_ref[half]
            down = up.T
            odd = jnp.broadcast_to(jnp.sum(d_ref[half], axis=0, keepdims=True), (128, 128))
            a = 256 * half
            g_ref[a : a + 128, a : a + 128] = jnp.where(row <= col, up, down)
            g_ref[a + 128 : a + 256, a + 128 : a + 256] = jnp.where(row > col, up, jnp.where(row < col, down, odd))

    for i in range(4):
        for j in range(i + 1, 4):
            g_ref[128 * j : 128 * j + 128, 128 * i : 128 * i + 128] = g_ref[
                128 * i : 128 * i + 128, 128 * j : 128 * j + 128
            ].T
    gram = g_ref[...]
    n = gram.shape[0]
    diag = lax.broadcasted_iota(jnp.int32, (n, n), 0) == lax.broadcasted_iota(jnp.int32, (n, n), 1)
    trace = jnp.sum(jnp.where(diag, gram, 0.0), keepdims=True)
    scale = 1.0 / (jnp.sqrt(trace) + 1e-07)
    g = gram * scale * scale
    gs = split(g)
    p1 = jnp.where(diag, A1, 0.0) + B1 * g + C1 * mm(gs, gs)
    p1s = split(p1)
    g2 = mm(split(mm(gs, p1s)), p1s)
    g2s = split(g2)
    p2 = jnp.where(diag, A1, 0.0) + B1 * g2 + C1 * mm(g2s, g2s)
    qs = split(mm(p1s, split(p2)) * (scale * jnp.sqrt(F32(ROWS))))
    copies = []
    for k, (a, b) in enumerate(row_cuts(hi.shape[0])):
        acc[a:b, :] = mm((hi[a:b, :], lo[a:b, :]), qs)
        copies.append(pltpu.make_async_copy(acc.at[pl.ds(a, b - a)], out.at[pl.ds(a, b - a)], sem.at[k]))
        copies[k].start()
    for copy in copies:
        copy.wait()


def apply(hi, lo, parts):
    return pl.pallas_call(
        apply_kernel,
        out_shape=jax.ShapeDtypeStruct(hi.shape, F32),
        in_specs=[VMEM] * (2 + len(parts)),
        out_specs=HBM,
        scratch_shapes=[
            pltpu.VMEM((512, 512), F32),
            pltpu.VMEM((2, 128, 128), F32),
            pltpu.VMEM((2, 32, 128), F32),
            pltpu.VMEM(hi.shape, F32),
            pltpu.SemaphoreType.DMA((3,)),
        ],
        compiler_params=params(),
        name="newton_schulz",
    )(near(hi), near(lo), *map(near, parts))


def swap(x, axis, size, bit):
    return lax.ppermute(x, axis, [(i, i ^ bit) for i in range(size)])


def over_x(x):
    return swap(x, "dp", 4, 1)


def over_y(x):
    return swap(x, "dp", 4, 2)


def over_core(x):
    return swap(x, "shard", 8, 1)


def over_z(x, r):
    return swap(x, "shard", 8, 2 * r)


def chunk_pair(a, b):
    def chunks():
        dp = lax.axis_index("dp")
        return [dp ^ a], [dp ^ b]

    return chunks


def body_4x8(layer_input, cotangent, momentum):
    chans = momentum.shape[0] // TAPS
    cp = layer_input.shape[0]
    taps = 7
    a3, b3, cot, v = conv(layer_input, cotangent, chunk_pair(3, 3), 1, taps)
    a3, b3 = over_x(a3), over_y(b3)
    a1, b1 = conv_more(cot, v, chunk_pair(1, 2), 1, taps, cp)
    a1, b1 = over_x(a1), over_y(b1)
    a2, b2 = conv_more(cot, v, chunk_pair(2, 1), 1, taps, cp)
    a2, b2 = over_y(a2 + a3), over_x(b2 + b3)
    a0, b0 = conv_more(cot, v, chunk_pair(0, 0), 1, taps, cp)
    own = own_momentum(momentum, taps, cp)
    m = momentum_update(own, (a0, b0, a1, b1, a2, b2), taps, cp)
    mx, my = over_x(m), over_y(m)
    keep, send = own_gram(m)
    g = keep + over_core(send)
    z3, z2, z1 = [over_z(g[r], r) for r in (3, 2, 1)]
    g = (z3 + z2) + (z1 + g[0])
    d3, d1, d2 = [swap(g, "dp", 4, r) for r in (3, 1, 2)]
    g = (d3 + d2) + (d1 + g)
    z3, z2, z1 = [over_z(g, r) for r in (3, 2, 1)]
    g = [z3, z2, z1, g]
    g = g + [over_core(x) for x in g]
    rows = taps * cp
    ad, bd = over_y(mx[:rows]), over_x(my[rows:])
    momentum_new, hi, lo = order((m, m, mx, mx, my, my, ad, bd), taps, cp, chans, True)
    return momentum_new, apply(hi, lo, g)


def body_any(n_dp, layer_input, cotangent, momentum):
    chans = layer_input.shape[0]
    cp = -(-chans // 16) * 16
    taps = -(-TAPS // n_dp)
    x = jnp.pad(layer_input, ((0, cp - chans), (0, 0)))
    part = conv(x, cotangent, lambda: [list(range(n_dp))] * 2, n_dp, taps)[:2]
    grad = [lax.psum_scatter(p, "dp", scatter_dimension=0, tiled=True) for p in part]
    m = momentum_update(own_momentum(momentum, taps, cp), grad, taps, cp)
    gram = lax.psum(any_gram(m), ("dp", "shard"))
    rows = taps * cp
    full = [lax.all_gather(half, "dp", axis=0, tiled=True) for half in (m[:rows], m[rows:])]
    momentum_new, hi, lo = order(full, taps, cp, chans, False)
    return momentum_new, apply(hi, lo, [gram])


def solution(mesh):
    n_dp = mesh.shape["dp"]
    known = (n_dp, mesh.shape["shard"]) == (4, 8)
    return jax.shard_map(
        body_4x8 if known else functools.partial(body_any, n_dp),
        mesh=mesh,
        in_specs=(P("shard", "dp"), P("dp", None), P("shard", None)),
        out_specs=(P("shard", None), P("shard", None)),
        check_vma=False,
    )
```

```python
import functools

import jax
import jax.numpy as jnp
from jax import lax
from jax.experimental import pallas as pl
from jax.experimental.pallas import tpu as pltpu
from jax.sharding import PartitionSpec as P

HW = 32
ROWS = 10368
PW = HW + 2
LANE = 128
TAPS = 27
A1, B1, C1 = 3.4445, -4.775, 2.0315
F32 = jnp.float32
BF16 = jnp.bfloat16
VMEM = pl.BlockSpec(memory_space=pltpu.VMEM)
HBM = pl.BlockSpec(memory_space=pltpu.HBM)
BLOCKS = (((0, 1), (0, 2), (0, 3)), ((1, 2), (1, 3), (2, 3)))
PIECE = (136, 128)


def column(rows):
    return pl.BlockSpec((rows, LANE), lambda c: (0, c))


def params(mib=24):
    return pltpu.CompilerParams(vmem_limit_bytes=mib << 20)


def near(x):
    return pltpu.with_memory_space_constraint(x, pltpu.VMEM)


def far(x):
    return pltpu.with_memory_space_constraint(x, pltpu.HBM)


def pair(tile, p, lane):
    t, c = divmod(p, LANE)
    if c + 64 <= LANE:
        return jnp.where(lane < c + 32, tile(t), tile(t + 4))
    if c + 32 <= LANE:
        far = jnp.where(lane < c, tile(t + 5), tile(t))
        if c + 32 == LANE:
            return far
        return jnp.where(lane < c + 32, far, tile(t + 4))
    near = jnp.where(lane < c + 32 - LANE, tile(t + 1), tile(t + 5))
    return jnp.where(lane < c, near, tile(t))


def build_slab(d0, half, g, xs, tail, v, cp):
    lane = lax.broadcasted_iota(jnp.int32, (16, LANE), 1)
    last = xs.shape[1] // LANE
    rows = slice(16 * g, 16 * g + 16)

    def tile(t):
        return tail[rows, :] if t == last else xs[rows, LANE * t : LANE * t + LANE]

    for j in range(18):
        for kw in range(3):
            part = []
            for s1 in range(2):
                p = (d0 + half * s1) * PW * PW + PW * j + kw
                part.append(pltpu.roll(pair(tile, p, lane), (64 * s1 - p) % LANE, 1))
            r0 = (d0 * 3 + kw) * cp + 16 * g
            v[r0 : r0 + 16, LANE * j : LANE * j + LANE] = jnp.where(lane < 64, part[0], part[1])


def conv_part(d, half, taps, cp, qs, cot, v, outs):
    vox = HW * HW
    for c in range(2):
        lhs = []
        for q in qs[c]:
            for i in range(taps):
                t = jnp.minimum(q * taps + i, TAPS - 1)
                kd, kh, kw = t // 9, t // 3 % 3, t % 3
                r0 = pl.multiple_of(((d + kd) * 3 + kw) * cp, 16)
                lhs.append(v[pl.ds(r0, cp), pl.ds(pl.multiple_of(LANE * kh, LANE), 16 * LANE)])
        rhs = []
        for h in range(16):
            for s1 in range(2):
                for s0 in range(2):
                    r0 = (d + half * s1) * vox + (h + 16 * s0) * HW
                    rhs.append(cot[r0 : r0 + HW, 256 * c : 256 * c + 256])
        part = jnp.dot(jnp.concatenate(lhs, 0), jnp.concatenate(rhs, 0), preferred_element_type=F32)
        if d == 0:
            outs[c][...] = part
        else:
            outs[c][...] += part


def conv_kernel(depth, cp, taps, chunks, x_hbm, cot_hbm, *refs):
    outs = refs[:2]
    cot, v, xs, tail, xsem, csem = refs[2:]
    half = depth // 2
    ln = xs.shape[1]
    vox = HW * HW
    groups = [pl.ds(16 * g, 16) for g in range(cp // 16)]
    xcopies = [pltpu.make_async_copy(x_hbm.at[r], xs.at[r], xsem.at[g]) for g, r in enumerate(groups)]
    for copy in xcopies:
        copy.start()
    copies = []
    for i in range(depth):
        rows = pl.ds(i * vox, vox)
        copies.append(pltpu.make_async_copy(cot_hbm.at[rows], cot.at[rows], csem.at[i]))
    n = ln // LANE * LANE
    for g, copy in enumerate(xcopies):
        copy.wait()
        if g == 0:
            for d in range(half):
                for s1 in range(2):
                    copies[d + half * s1].start()
        if n < ln:
            tail[16 * g : 16 * g + 16, : ln - n] = xs[16 * g : 16 * g + 16, n:]
        for d0 in range(half + 2):
            build_slab(d0, half, g, xs, tail, v, cp)
    qs = chunks()
    for d in range(half):
        for s1 in range(2):
            copies[d + half * s1].wait()
        conv_part(d, half, taps, cp, qs, cot, v, outs)


def conv(x, cot, chunks, slots, taps):
    cp, ln = x.shape
    depth = cot.shape[0] // (HW * HW)
    return pl.pallas_call(
        functools.partial(conv_kernel, depth, cp, taps, chunks),
        out_shape=[pltpu.VMEM((slots * taps * cp, 256), F32)] * 2
        + [pltpu.VMEM(cot.shape, BF16), pltpu.VMEM((3 * (depth // 2 + 2) * cp, 18 * LANE), BF16)],
        in_specs=[HBM, HBM],
        out_specs=[VMEM] * 4,
        scratch_shapes=[
            pltpu.VMEM((cp, ln), BF16),
            pltpu.VMEM((cp, LANE), BF16),
            pltpu.SemaphoreType.DMA((cp // 16,)),
            pltpu.SemaphoreType.DMA((depth,)),
        ],
        compiler_params=params(),
        name="conv_first",
    )(far(x), far(cot))


def more_kernel(depth, cp, taps, chunks, cot, v, *outs):
    qs = chunks()
    for d in range(depth // 2):
        conv_part(d, depth // 2, taps, cp, qs, cot, v, outs)


def conv_more(cot, v, chunks, slots, taps, cp):
    depth = cot.shape[0] // (HW * HW)
    return pl.pallas_call(
        functools.partial(more_kernel, depth, cp, taps, chunks),
        out_shape=[pltpu.VMEM((slots * taps * cp, 256), F32)] * 2,
        in_specs=[VMEM] * 2,
        out_specs=[VMEM] * 2,
        compiler_params=params(),
        name="conv_more",
    )(near(cot), near(v))


def own_kernel(taps, cp, m_ref, o_ref):
    chans = m_ref.shape[0] // TAPS
    for i in range(taps):
        t = lax.axis_index("dp") * taps + i
        rows = m_ref[pl.ds(jnp.minimum(t, TAPS - 1), chans, stride=TAPS), :]
        o_ref[cp * i : cp * i + chans, :] = jnp.where(t < TAPS, rows, 0.0)
        if cp > chans:
            o_ref[cp * i + chans : cp * i + cp, :] = jnp.zeros((cp - chans, LANE), F32)


def own_momentum(momentum, taps, cp):
    return pl.pallas_call(
        functools.partial(own_kernel, taps, cp),
        out_shape=jax.ShapeDtypeStruct((taps * cp, momentum.shape[1]), F32),
        grid=(momentum.shape[1] // LANE,),
        in_specs=[column(momentum.shape[0])],
        out_specs=column(taps * cp),
        compiler_params=params(),
        name="own_momentum",
    )(momentum)


def split(x):
    hi = x.astype(BF16)
    return hi, (x - hi.astype(F32)).astype(BF16)


def dot_t(a, b):
    return lax.dot_general(a, b, (((0,), (0,)), ((), ())), preferred_element_type=F32)


def update(m, grad, taps, cp):
    tap = lax.axis_index("dp") * taps + lax.broadcasted_iota(jnp.int32, (taps * cp, 1), 0) // cp
    return jnp.where(tap < TAPS, 0.95 * m + grad, 0.0)


def update_kernel(taps, cp, m_ref, *refs):
    parts, out = refs[:-1], refs[-1]
    rows = taps * cp
    for c in range(2):
        grad = parts[c][...]
        for n in range(2 + c, len(parts), 2):
            grad = grad + parts[n][...]
        out[rows * c : rows * c + rows, :] = update(m_ref[:, 256 * c : 256 * c + 256], grad, taps, cp)


def momentum_update(own, parts, taps, cp):
    return pl.pallas_call(
        functools.partial(update_kernel, taps, cp),
        out_shape=pltpu.VMEM((2 * taps * cp, 256), F32),
        in_specs=[VMEM] * (1 + len(parts)),
        out_specs=VMEM,
        compiler_params=params(),
        name="momentum_update",
    )(near(own), *map(near, parts))


def upper_gram(m):
    hi, lo = split(m)
    out = []
    for i in range(4):
        a, b = slice(128 * i, 128 * i + 128), slice(128 * i, 512)
        out.append(dot_t(hi[:, a], hi[:, b]) + (dot_t(hi[:, a], lo[:, b]) + dot_t(lo[:, a], hi[:, b])))
    return out


def gram_kernel(m, keep, send):
    z, core = lax.axis_index("shard") // 2, lax.axis_index("shard") % 2
    rows = m.shape[0] // 2
    gram = upper_gram(jnp.concatenate([m[:rows], m[rows:]], 1))
    row = lax.broadcasted_iota(jnp.int32, (128, 128), 0)
    col = lax.broadcasted_iota(jnp.int32, (128, 128), 1)
    for half in range(2):
        blocks = [gram[i][:, 128 * (j - i) : 128 * (j - i) + 128] for i, j in BLOCKS[half]]
        even, odd = gram[2 * half][:, :128], gram[2 * half + 1][:, :128]
        blocks.append(jnp.where(row <= col, even, odd))
        diag = jnp.where(row == col, odd, 0.0)
        for r in range(4):
            cut = slice(32 * r, 32 * r + 32)
            last = jnp.sum(diag[cut], axis=0, keepdims=True)
            last = jnp.where(row[:8] == 0, jnp.broadcast_to(last, (8, 128)), 0.0)
            piece = jnp.concatenate([block[cut] for block in blocks] + [last], 0)

            @pl.when(core == half)
            def _():
                keep[r ^ z] = piece

            @pl.when(core != half)
            def _():
                send[r ^ z] = piece


def own_gram(m):
    return pl.pallas_call(
        gram_kernel,
        out_shape=[pltpu.VMEM((4,) + PIECE, F32)] * 2,
        in_specs=[VMEM],
        out_specs=[VMEM] * 2,
        compiler_params=params(),
        name="own_gram",
    )(near(m))


def any_gram_kernel(m, g_ref):
    half = m.shape[0] // 2
    for i, rows in enumerate(upper_gram(jnp.concatenate([m[:half], m[half:]], 1))):
        g_ref[128 * i : 128 * i + 128, :] = jnp.zeros((128, 512), F32)
        g_ref[128 * i : 128 * i + 128, 128 * i :] = rows


def any_gram(m):
    return pl.pallas_call(
        any_gram_kernel,
        out_shape=jax.ShapeDtypeStruct((512, 512), F32),
        in_specs=[VMEM],
        out_specs=VMEM,
        compiler_params=params(),
        name="own_gram",
    )(near(m))


def second_kernel(more, m, mx, my, nx, ny):
    rows = m.shape[0] // 2
    nx[: rows - more, :] = m[rows + more :, :]
    nx[rows - more :, :] = my[more:, :]
    ny[: rows - more, :] = m[: rows - more, :]
    ny[rows - more :, :] = mx[:rows, :]


def second_step(m, mx, my, more):
    return pl.pallas_call(
        functools.partial(second_kernel, more),
        out_shape=[pltpu.VMEM((m.shape[0] - more, 256), F32)] * 2,
        in_specs=[VMEM] * 3,
        out_specs=[VMEM] * 2,
        compiler_params=params(),
        name="second_step",
    )(near(m), near(mx), near(my))


def mm(a, b):
    ah, al = a
    bh, bl = b
    d = functools.partial(jnp.dot, preferred_element_type=F32)
    return d(ah, bh) + (d(ah, bl) + d(al, bh))


def poly_kernel(*refs):
    parts, (qh, ql, g_ref, p_ref, d_ref) = refs[:-5], refs[-5:]
    if len(parts) == 1:
        g_ref[...] = parts[0][...]
    else:
        z, core = lax.axis_index("shard") // 2, lax.axis_index("shard") % 2
        for n, part in enumerate(parts):
            which, r = n // 4, 3 - n % 4
            q = z ^ r
            for half in range(2):

                @pl.when(core ^ which == half)
                def _():
                    for k, (i, j) in enumerate(BLOCKS[half]):
                        rows = pl.ds(pl.multiple_of(128 * i + 32 * q, 32), 32)
                        g_ref[rows, 128 * j : 128 * j + 128] = part[32 * k : 32 * k + 32]
                    p_ref[half, pl.ds(pl.multiple_of(32 * q, 32), 32), :] = part[96:128]
                    d_ref[half, 8 * r : 8 * r + 8, :] = part[128:136]

        row = lax.broadcasted_iota(jnp.int32, (128, 128), 0)
        col = lax.broadcasted_iota(jnp.int32, (128, 128), 1)
        for half in range(2):
            up = p_ref[half]
            down = up.T
            odd = jnp.broadcast_to(jnp.sum(d_ref[half], axis=0, keepdims=True), (128, 128))
            a = 256 * half
            g_ref[a : a + 128, a : a + 128] = jnp.where(row <= col, up, down)
            g_ref[a + 128 : a + 256, a + 128 : a + 256] = jnp.where(row > col, up, jnp.where(row < col, down, odd))

    for i in range(4):
        for j in range(i + 1, 4):
            g_ref[128 * j : 128 * j + 128, 128 * i : 128 * i + 128] = g_ref[
                128 * i : 128 * i + 128, 128 * j : 128 * j + 128
            ].T
    gram = g_ref[...]
    n = gram.shape[0]
    diag = lax.broadcasted_iota(jnp.int32, (n, n), 0) == lax.broadcasted_iota(jnp.int32, (n, n), 1)
    trace = jnp.sum(jnp.where(diag, gram, 0.0), keepdims=True)
    scale = 1.0 / (jnp.sqrt(trace) + 1e-07)
    g = gram * scale * scale
    gs = split(g)
    p1 = jnp.where(diag, A1, 0.0) + B1 * g + C1 * mm(gs, gs)
    p1s = split(p1)
    g2 = mm(split(mm(gs, p1s)), p1s)
    g2s = split(g2)
    p2 = jnp.where(diag, A1, 0.0) + B1 * g2 + C1 * mm(g2s, g2s)
    qh[...], ql[...] = split(mm(p1s, split(p2)) * (scale * jnp.sqrt(F32(ROWS))))


def newton_schulz(parts):
    return pl.pallas_call(
        poly_kernel,
        out_shape=[pltpu.VMEM((512, 512), BF16)] * 2,
        in_specs=[VMEM] * len(parts),
        out_specs=[VMEM] * 2,
        scratch_shapes=[
            pltpu.VMEM((512, 512), F32),
            pltpu.VMEM((2, 128, 128), F32),
            pltpu.VMEM((2, 32, 128), F32),
        ],
        compiler_params=params(),
        name="newton_schulz",
    )(*map(near, parts))


def finish_kernel(taps, cp, chans, known, places, qh, ql, *refs):
    parts, (new, out, cols, hi, lo, acc, sem, osem) = refs[:-8], refs[-8:]
    copies = []
    for c in range(4):
        for r in range(len(places) // 2):
            i = 0
            for n, base in places[2 * r + c // 2]:
                ends = [b for m, b in sum(places, []) if m == n and b > base] + [parts[n].shape[0]]
                for at in range(base, min(ends), cp):
                    if i >= taps:
                        break
                    t = (lax.axis_index("dp") ^ r) * taps + i if known else r * taps + i
                    i += 1
                    if not known and t >= TAPS:
                        continue
                    rows = parts[n][at : at + chans, LANE * (c % 2) : LANE * (c % 2) + LANE]

                    @pl.when(t < TAPS)
                    def _():
                        cols.at[c][pl.ds(t, chans, stride=TAPS), :] = rows

            assert i == taps
        copies.append(pltpu.make_async_copy(cols.at[c], new.at[:, pl.ds(LANE * c, LANE)], sem.at[c]))
        copies[c].start()
        hi[:, LANE * c : LANE * c + LANE], lo[:, LANE * c : LANE * c + LANE] = split(cols[c])
    for k, (a, b) in enumerate(row_cuts(acc.shape[0])):
        acc[a:b, :] = mm((hi[a:b, :], lo[a:b, :]), (qh[...], ql[...]))
        copies.append(pltpu.make_async_copy(acc.at[pl.ds(a, b - a)], out.at[pl.ds(a, b - a)], osem.at[k]))
        copies[-1].start()
    for copy in copies:
        copy.wait()


def row_cuts(rows):
    cuts = [min(rows, -(-rows * k // 24) * 8) for k in range(4)]
    return [(a, b) for a, b in zip(cuts, cuts[1:]) if b > a]


def finish(q, parts, places, taps, cp, chans, known):
    rows = chans * TAPS
    return pl.pallas_call(
        functools.partial(finish_kernel, taps, cp, chans, known, list(places)),
        out_shape=[jax.ShapeDtypeStruct((rows, 512), F32)] * 2,
        in_specs=[VMEM] * (2 + len(parts)),
        out_specs=[HBM] * 2,
        scratch_shapes=[
            pltpu.VMEM((4, rows, LANE), F32),
            pltpu.VMEM((rows, 512), BF16),
            pltpu.VMEM((rows, 512), BF16),
            pltpu.VMEM((rows, 512), F32),
            pltpu.SemaphoreType.DMA((4,)),
            pltpu.SemaphoreType.DMA((3,)),
        ],
        compiler_params=params(),
        name="finish",
    )(*map(near, q), *map(near, parts))


def swap(x, axis, size, bit):
    return lax.ppermute(x, axis, [(i, i ^ bit) for i in range(size)])


def over_x(x):
    return swap(x, "dp", 4, 1)


def over_y(x):
    return swap(x, "dp", 4, 2)


def over_core(x):
    return swap(x, "shard", 8, 1)


def over_z(x, r):
    return swap(x, "shard", 8, 2 * r)


def chunk_pair(a, b):
    def chunks():
        dp = lax.axis_index("dp")
        return [dp ^ a], [dp ^ b]

    return chunks


def body_4x8(layer_input, cotangent, momentum):
    chans = momentum.shape[0] // TAPS
    cp = layer_input.shape[0]
    taps = 7
    a3, b3, cot, v = conv(layer_input, cotangent, chunk_pair(3, 3), 1, taps)
    a3, b3 = over_x(a3), over_y(b3)
    a1, b1 = conv_more(cot, v, chunk_pair(1, 2), 1, taps, cp)
    a1, b1 = over_x(a1), over_y(b1)
    a2, b2 = conv_more(cot, v, chunk_pair(2, 1), 1, taps, cp)
    a2, b2 = over_y(a2 + a3), over_x(b2 + b3)
    a0, b0 = conv_more(cot, v, chunk_pair(0, 0), 1, taps, cp)
    own = own_momentum(momentum, taps, cp)
    m = momentum_update(own, (a0, b0, a1, b1, a2, b2), taps, cp)
    rows = taps * cp
    more = 4 * cp
    mx, my = over_x(m[: rows + more]), over_y(m[rows - more :])
    keep, send = own_gram(m)
    g = keep + over_core(send)
    z3, z2, z1 = [over_z(g[r], r) for r in (3, 2, 1)]
    g = (z3 + z2) + (z1 + g[0])
    d3, d1, d2 = [swap(g, "dp", 4, r) for r in (3, 1, 2)]
    g = (d3 + d2) + (d1 + g)
    z3, z2, z1 = [over_z(g, r) for r in (3, 2, 1)]
    g = [z3, z2, z1, g]
    g = g + [over_core(x) for x in g]
    nx, ny = second_step(m, mx, my, more)
    nx, ny = over_x(nx), over_y(ny)
    rest = rows - more
    places = (
        [(0, 0)], [(0, rows)],
        [(1, 0)], [(1, rows), (3, 0)],
        [(4, 0), (2, 0)], [(2, more)],
        [(4, rest)], [(3, rest)],
    )
    return finish(newton_schulz(g), (m, mx, my, nx, ny), places, taps, cp, chans, True)


def body_any(n_dp, layer_input, cotangent, momentum):
    chans = layer_input.shape[0]
    cp = -(-chans // 16) * 16
    taps = -(-TAPS // n_dp)
    x = jnp.pad(layer_input, ((0, cp - chans), (0, 0)))
    part = conv(x, cotangent, lambda: [list(range(n_dp))] * 2, n_dp, taps)[:2]
    grad = [lax.psum_scatter(p, "dp", scatter_dimension=0, tiled=True) for p in part]
    m = momentum_update(own_momentum(momentum, taps, cp), grad, taps, cp)
    gram = lax.psum(any_gram(m), ("dp", "shard"))
    rows = taps * cp
    full = [lax.all_gather(half, "dp", axis=0, tiled=True) for half in (m[:rows], m[rows:])]
    places = [[(half, r * rows)] for r in range(n_dp) for half in range(2)]
    return finish(newton_schulz([gram]), full, places, taps, cp, chans, False)


def solution(mesh):
    n_dp = mesh.shape["dp"]
    known = (n_dp, mesh.shape["shard"]) == (4, 8)
    return jax.shard_map(
        body_4x8 if known else functools.partial(body_any, n_dp),
        mesh=mesh,
        in_specs=(P("shard", "dp"), P("dp", None), P("shard", None)),
        out_specs=(P("shard", None), P("shard", None)),
        check_vma=False,
    )
```

```python
import functools

import jax
import jax.numpy as jnp
from jax import lax
from jax.experimental import pallas as pl
from jax.experimental.pallas import tpu as pltpu
from jax.sharding import PartitionSpec as P

HW = 32
ROWS = 10368
PW = HW + 2
LANE = 128
TAPS = 27
A1, B1, C1 = 3.4445, -4.775, 2.0315
F32 = jnp.float32
BF16 = jnp.bfloat16
VMEM = pl.BlockSpec(memory_space=pltpu.VMEM)
HBM = pl.BlockSpec(memory_space=pltpu.HBM)
BLOCKS = (((0, 1), (0, 2), (0, 3)), ((1, 2), (1, 3), (2, 3)))
PIECE = (136, 128)


def column(rows):
    return pl.BlockSpec((rows, LANE), lambda c: (0, c))


def params(mib=24):
    return pltpu.CompilerParams(vmem_limit_bytes=mib << 20)


def near(x):
    return pltpu.with_memory_space_constraint(x, pltpu.VMEM)


def far(x):
    return pltpu.with_memory_space_constraint(x, pltpu.HBM)


def pair(tile, p, lane):
    t, c = divmod(p, LANE)
    if c + 64 <= LANE:
        return jnp.where(lane < c + 32, tile(t), tile(t + 4))
    if c + 32 <= LANE:
        far = jnp.where(lane < c, tile(t + 5), tile(t))
        if c + 32 == LANE:
            return far
        return jnp.where(lane < c + 32, far, tile(t + 4))
    near = jnp.where(lane < c + 32 - LANE, tile(t + 1), tile(t + 5))
    return jnp.where(lane < c, near, tile(t))


def build_slab(d0, half, g, xs, tail, v, cp):
    lane = lax.broadcasted_iota(jnp.int32, (16, LANE), 1)
    last = xs.shape[1] // LANE
    rows = slice(16 * g, 16 * g + 16)

    def tile(t):
        return tail[rows, :] if t == last else xs[rows, LANE * t : LANE * t + LANE]

    for j in range(18):
        for kw in range(3):
            part = []
            for s1 in range(2):
                p = (d0 + half * s1) * PW * PW + PW * j + kw
                part.append(pltpu.roll(pair(tile, p, lane), (64 * s1 - p) % LANE, 1))
            r0 = (d0 * 3 + kw) * cp + 16 * g
            v[r0 : r0 + 16, LANE * j : LANE * j + LANE] = jnp.where(lane < 64, part[0], part[1])


def conv_part(d, half, taps, cp, qs, cot, v, outs):
    vox = HW * HW
    for c in range(2):
        lhs = []
        for q in qs[c]:
            for i in range(taps):
                t = jnp.minimum(q * taps + i, TAPS - 1)
                kd, kh, kw = t // 9, t // 3 % 3, t % 3
                r0 = pl.multiple_of(((d + kd) * 3 + kw) * cp, 16)
                lhs.append(v[pl.ds(r0, cp), pl.ds(pl.multiple_of(LANE * kh, LANE), 16 * LANE)])
        rhs = []
        for h in range(16):
            for s1 in range(2):
                for s0 in range(2):
                    r0 = (d + half * s1) * vox + (h + 16 * s0) * HW
                    rhs.append(cot[r0 : r0 + HW, 256 * c : 256 * c + 256])
        part = jnp.dot(jnp.concatenate(lhs, 0), jnp.concatenate(rhs, 0), preferred_element_type=F32)
        if d == 0:
            outs[c][...] = part
        else:
            outs[c][...] += part


def conv_kernel(depth, cp, taps, chunks, x_hbm, cot_hbm, *refs):
    outs = refs[:2]
    cot, v, xs, tail, xsem, csem = refs[2:]
    half = depth // 2
    ln = xs.shape[1]
    vox = HW * HW
    groups = [pl.ds(16 * g, 16) for g in range(cp // 16)]
    xcopies = [pltpu.make_async_copy(x_hbm.at[r], xs.at[r], xsem.at[g]) for g, r in enumerate(groups)]
    for copy in xcopies:
        copy.start()
    copies = []
    for i in range(depth):
        rows = pl.ds(i * vox, vox)
        copies.append(pltpu.make_async_copy(cot_hbm.at[rows], cot.at[rows], csem.at[i]))
    n = ln // LANE * LANE
    for g, copy in enumerate(xcopies):
        copy.wait()
        if g == 0:
            for d in range(half):
                for s1 in range(2):
                    copies[d + half * s1].start()
        if n < ln:
            tail[16 * g : 16 * g + 16, : ln - n] = xs[16 * g : 16 * g + 16, n:]
        for d0 in range(half + 2):
            build_slab(d0, half, g, xs, tail, v, cp)
    qs = chunks()
    for d in range(half):
        for s1 in range(2):
            copies[d + half * s1].wait()
        conv_part(d, half, taps, cp, qs, cot, v, outs)


def conv(x, cot, chunks, slots, taps):
    cp, ln = x.shape
    depth = cot.shape[0] // (HW * HW)
    return pl.pallas_call(
        functools.partial(conv_kernel, depth, cp, taps, chunks),
        out_shape=[pltpu.VMEM((slots * taps * cp, 256), F32)] * 2
        + [pltpu.VMEM(cot.shape, BF16), pltpu.VMEM((3 * (depth // 2 + 2) * cp, 18 * LANE), BF16)],
        in_specs=[HBM, HBM],
        out_specs=[VMEM] * 4,
        scratch_shapes=[
            pltpu.VMEM((cp, ln), BF16),
            pltpu.VMEM((cp, LANE), BF16),
            pltpu.SemaphoreType.DMA((cp // 16,)),
            pltpu.SemaphoreType.DMA((depth,)),
        ],
        compiler_params=params(),
        name="conv_first",
    )(far(x), far(cot))


def more_kernel(depth, cp, taps, chunks, cot, v, *outs):
    qs = chunks()
    for d in range(depth // 2):
        conv_part(d, depth // 2, taps, cp, qs, cot, v, outs)


def conv_more(cot, v, chunks, slots, taps, cp):
    depth = cot.shape[0] // (HW * HW)
    return pl.pallas_call(
        functools.partial(more_kernel, depth, cp, taps, chunks),
        out_shape=[pltpu.VMEM((slots * taps * cp, 256), F32)] * 2,
        in_specs=[VMEM] * 2,
        out_specs=[VMEM] * 2,
        compiler_params=params(),
        name="conv_more",
    )(near(cot), near(v))


def own_kernel(taps, cp, m_ref, o_ref):
    chans = m_ref.shape[0] // TAPS
    for i in range(taps):
        t = lax.axis_index("dp") * taps + i
        rows = m_ref[pl.ds(jnp.minimum(t, TAPS - 1), chans, stride=TAPS), :]
        o_ref[cp * i : cp * i + chans, :] = jnp.where(t < TAPS, rows, 0.0)
        if cp > chans:
            o_ref[cp * i + chans : cp * i + cp, :] = jnp.zeros((cp - chans, LANE), F32)


def own_momentum(momentum, taps, cp):
    return pl.pallas_call(
        functools.partial(own_kernel, taps, cp),
        out_shape=jax.ShapeDtypeStruct((taps * cp, momentum.shape[1]), F32),
        grid=(momentum.shape[1] // LANE,),
        in_specs=[column(momentum.shape[0])],
        out_specs=column(taps * cp),
        compiler_params=params(),
        name="own_momentum",
    )(momentum)


def split(x):
    hi = x.astype(BF16)
    return hi, (x - hi.astype(F32)).astype(BF16)


def dot_t(a, b):
    return lax.dot_general(a, b, (((0,), (0,)), ((), ())), preferred_element_type=F32)


def update(m, grad, taps, cp):
    tap = lax.axis_index("dp") * taps + lax.broadcasted_iota(jnp.int32, (taps * cp, 1), 0) // cp
    return jnp.where(tap < TAPS, 0.95 * m + grad, 0.0)


def update_kernel(taps, cp, m_ref, *refs):
    parts, out = refs[:-1], refs[-1]
    rows = taps * cp
    for c in range(2):
        grad = parts[c][...]
        for n in range(2 + c, len(parts), 2):
            grad = grad + parts[n][...]
        out[rows * c : rows * c + rows, :] = update(m_ref[:, 256 * c : 256 * c + 256], grad, taps, cp)


def momentum_update(own, parts, taps, cp):
    return pl.pallas_call(
        functools.partial(update_kernel, taps, cp),
        out_shape=pltpu.VMEM((2 * taps * cp, 256), F32),
        in_specs=[VMEM] * (1 + len(parts)),
        out_specs=VMEM,
        compiler_params=params(),
        name="momentum_update",
    )(near(own), *map(near, parts))


def upper_gram(m):
    hi, lo = split(m)
    out = []
    for i in range(4):
        a, b = slice(128 * i, 128 * i + 128), slice(128 * i, 512)
        out.append(dot_t(hi[:, a], hi[:, b]) + (dot_t(hi[:, a], lo[:, b]) + dot_t(lo[:, a], hi[:, b])))
    return out


def gram_kernel(m, keep, send):
    z, core = lax.axis_index("shard") // 2, lax.axis_index("shard") % 2
    rows = m.shape[0] // 2
    gram = upper_gram(jnp.concatenate([m[:rows], m[rows:]], 1))
    row = lax.broadcasted_iota(jnp.int32, (128, 128), 0)
    col = lax.broadcasted_iota(jnp.int32, (128, 128), 1)
    for half in range(2):
        blocks = [gram[i][:, 128 * (j - i) : 128 * (j - i) + 128] for i, j in BLOCKS[half]]
        even, odd = gram[2 * half][:, :128], gram[2 * half + 1][:, :128]
        blocks.append(jnp.where(row <= col, even, odd))
        diag = jnp.where(row == col, odd, 0.0)
        for r in range(4):
            cut = slice(32 * r, 32 * r + 32)
            last = jnp.sum(diag[cut], axis=0, keepdims=True)
            last = jnp.where(row[:8] == 0, jnp.broadcast_to(last, (8, 128)), 0.0)
            piece = jnp.concatenate([block[cut] for block in blocks] + [last], 0)

            @pl.when(core == half)
            def _():
                keep[r ^ z] = piece

            @pl.when(core != half)
            def _():
                send[r ^ z] = piece


def own_gram(m):
    return pl.pallas_call(
        gram_kernel,
        out_shape=[pltpu.VMEM((4,) + PIECE, F32)] * 2,
        in_specs=[VMEM],
        out_specs=[VMEM] * 2,
        compiler_params=params(),
        name="own_gram",
    )(near(m))


def any_gram_kernel(m, g_ref):
    half = m.shape[0] // 2
    for i, rows in enumerate(upper_gram(jnp.concatenate([m[:half], m[half:]], 1))):
        g_ref[128 * i : 128 * i + 128, :] = jnp.zeros((128, 512), F32)
        g_ref[128 * i : 128 * i + 128, 128 * i :] = rows


def any_gram(m):
    return pl.pallas_call(
        any_gram_kernel,
        out_shape=jax.ShapeDtypeStruct((512, 512), F32),
        in_specs=[VMEM],
        out_specs=VMEM,
        compiler_params=params(),
        name="own_gram",
    )(near(m))


def second_kernel(more, m, mx, my, nx, ny):
    rows = m.shape[0] // 2
    nx[: rows - more, :] = m[rows + more :, :]
    nx[rows - more :, :] = my[more:, :]
    ny[: rows - more, :] = m[: rows - more, :]
    ny[rows - more :, :] = mx[:rows, :]


def second_step(m, mx, my, more):
    return pl.pallas_call(
        functools.partial(second_kernel, more),
        out_shape=[pltpu.VMEM((m.shape[0] - more, 256), F32)] * 2,
        in_specs=[VMEM] * 3,
        out_specs=[VMEM] * 2,
        compiler_params=params(),
        name="second_step",
    )(near(m), near(mx), near(my))


def mm(a, b):
    ah, al = a
    bh, bl = b
    d = functools.partial(jnp.dot, preferred_element_type=F32)
    return d(ah, bh) + (d(ah, bl) + d(al, bh))


def assemble(parts, g_ref, p_ref, d_ref):
    if len(parts) == 1:
        g_ref[...] = parts[0][...]
    else:
        z, core = lax.axis_index("shard") // 2, lax.axis_index("shard") % 2
        for n, part in enumerate(parts):
            which, r = n // 4, 3 - n % 4
            q = z ^ r
            for half in range(2):

                @pl.when(core ^ which == half)
                def _():
                    for k, (i, j) in enumerate(BLOCKS[half]):
                        rows = pl.ds(pl.multiple_of(128 * i + 32 * q, 32), 32)
                        g_ref[rows, 128 * j : 128 * j + 128] = part[32 * k : 32 * k + 32]
                    p_ref[half, pl.ds(pl.multiple_of(32 * q, 32), 32), :] = part[96:128]
                    d_ref[half, 8 * r : 8 * r + 8, :] = part[128:136]

        row = lax.broadcasted_iota(jnp.int32, (128, 128), 0)
        col = lax.broadcasted_iota(jnp.int32, (128, 128), 1)
        for half in range(2):
            up = p_ref[half]
            down = up.T
            odd = jnp.broadcast_to(jnp.sum(d_ref[half], axis=0, keepdims=True), (128, 128))
            a = 256 * half
            g_ref[a : a + 128, a : a + 128] = jnp.where(row <= col, up, down)
            g_ref[a + 128 : a + 256, a + 128 : a + 256] = jnp.where(row > col, up, jnp.where(row < col, down, odd))

    for i in range(4):
        for j in range(i + 1, 4):
            g_ref[128 * j : 128 * j + 128, 128 * i : 128 * i + 128] = g_ref[
                128 * i : 128 * i + 128, 128 * j : 128 * j + 128
            ].T


def tap_rows(places, parts, taps, cp, slot):
    out = []
    for n, base in places[slot]:
        ends = [b for m, b in sum(places, []) if m == n and b > base] + [parts[n].shape[0]]
        out += [(n, at) for at in range(base, min(ends), cp)]
    return out[:taps]


def row_cuts(rows):
    cuts = [min(rows, -(-rows * k // 24) * 8) for k in range(4)]
    return [(a, b) for a, b in zip(cuts, cuts[1:]) if b > a]


def finish_kernel(taps, cp, chans, known, places, count, *refs):
    parts, grams = refs[:count], refs[count:-11]
    new, out, g_ref, p_ref, d_ref, cols, hi, lo, acc, sem, osem = refs[-11:]
    copies = []

    def reorder(c):
        lanes = slice(LANE * (c % 2), LANE * (c % 2) + LANE)
        for r in range(len(places) // 2):
            rows = None
            for i, (n, at) in enumerate(tap_rows(places, parts, taps, cp, 2 * r + c // 2)):
                if not known and r * taps + i >= TAPS:
                    continue
                before, rows = rows, parts[n][at : at + chans, lanes]
                t = r * taps + i
                if known:
                    t = (lax.axis_index("dp") ^ r) * taps + i
                    if 3 * taps + i >= TAPS:
                        rows = jnp.where(t < TAPS, rows, before)
                        t = jnp.minimum(t, TAPS - 1)
                cols.at[c][pl.ds(t, chans, stride=TAPS), :] = rows
        hi[:, LANE * c : LANE * c + LANE], lo[:, LANE * c : LANE * c + LANE] = split(cols[c])
        copies.append(pltpu.make_async_copy(cols.at[c], new.at[:, pl.ds(LANE * c, LANE)], sem.at[c]))
        copies[-1].start()

    assemble(grams, g_ref, p_ref, d_ref)
    gram = g_ref[...]
    n = gram.shape[0]
    diag = lax.broadcasted_iota(jnp.int32, (n, n), 0) == lax.broadcasted_iota(jnp.int32, (n, n), 1)
    trace = jnp.sum(jnp.where(diag, gram, 0.0), keepdims=True)
    scale = 1.0 / (jnp.sqrt(trace) + 1e-07)
    g = gram * scale * scale
    gs = split(g)
    p1 = jnp.where(diag, A1, 0.0) + B1 * g + C1 * mm(gs, gs)
    reorder(0)
    p1s = split(p1)
    h = mm(gs, p1s)
    reorder(1)
    g2 = mm(split(h), p1s)
    reorder(2)
    g2s = split(g2)
    p2 = jnp.where(diag, A1, 0.0) + B1 * g2 + C1 * mm(g2s, g2s)
    reorder(3)
    qs = split(mm(p1s, split(p2)) * (scale * jnp.sqrt(F32(ROWS))))
    for k, (a, b) in enumerate(row_cuts(acc.shape[0])):
        acc[a:b, :] = mm((hi[a:b, :], lo[a:b, :]), qs)
        copies.append(pltpu.make_async_copy(acc.at[pl.ds(a, b - a)], out.at[pl.ds(a, b - a)], osem.at[k]))
        copies[-1].start()
    for copy in copies:
        copy.wait()


def finish(grams, parts, places, taps, cp, chans, known):
    rows = chans * TAPS
    return pl.pallas_call(
        functools.partial(finish_kernel, taps, cp, chans, known, list(places), len(parts)),
        out_shape=[jax.ShapeDtypeStruct((rows, 512), F32)] * 2,
        in_specs=[VMEM] * (len(grams) + len(parts)),
        out_specs=[HBM] * 2,
        scratch_shapes=[
            pltpu.VMEM((512, 512), F32),
            pltpu.VMEM((2, 128, 128), F32),
            pltpu.VMEM((2, 32, 128), F32),
            pltpu.VMEM((4, rows, LANE), F32),
            pltpu.VMEM((rows, 512), BF16),
            pltpu.VMEM((rows, 512), BF16),
            pltpu.VMEM((rows, 512), F32),
            pltpu.SemaphoreType.DMA((4,)),
            pltpu.SemaphoreType.DMA((3,)),
        ],
        compiler_params=params(),
        name="finish",
    )(*map(near, parts), *map(near, grams))


def swap(x, axis, size, bit):
    return lax.ppermute(x, axis, [(i, i ^ bit) for i in range(size)])


def over_x(x):
    return swap(x, "dp", 4, 1)


def over_y(x):
    return swap(x, "dp", 4, 2)


def over_core(x):
    return swap(x, "shard", 8, 1)


def over_z(x, r):
    return swap(x, "shard", 8, 2 * r)


def chunk_pair(a, b):
    def chunks():
        dp = lax.axis_index("dp")
        return [dp ^ a], [dp ^ b]

    return chunks


def body_4x8(layer_input, cotangent, momentum):
    chans = momentum.shape[0] // TAPS
    cp = layer_input.shape[0]
    taps = 7
    a3, b3, cot, v = conv(layer_input, cotangent, chunk_pair(3, 3), 1, taps)
    a3, b3 = over_x(a3), over_y(b3)
    a1, b1 = conv_more(cot, v, chunk_pair(1, 2), 1, taps, cp)
    a1, b1 = over_x(a1), over_y(b1)
    a2, b2 = conv_more(cot, v, chunk_pair(2, 1), 1, taps, cp)
    a2, b2 = over_y(a2 + a3), over_x(b2 + b3)
    a0, b0 = conv_more(cot, v, chunk_pair(0, 0), 1, taps, cp)
    own = own_momentum(momentum, taps, cp)
    m = momentum_update(own, (a0, b0, a1, b1, a2, b2), taps, cp)
    rows = taps * cp
    more = 4 * cp
    mx, my = over_x(m[: rows + more]), over_y(m[rows - more :])
    keep, send = own_gram(m)
    g = keep + over_core(send)
    z3, z2, z1 = [over_z(g[r], r) for r in (3, 2, 1)]
    g = (z3 + z2) + (z1 + g[0])
    d3, d1, d2 = [swap(g, "dp", 4, r) for r in (3, 1, 2)]
    g = (d3 + d2) + (d1 + g)
    z3, z2, z1 = [over_z(g, r) for r in (3, 2, 1)]
    g = [z3, z2, z1, g]
    g = g + [over_core(x) for x in g]
    nx, ny = second_step(m, mx, my, more)
    nx, ny = over_x(nx), over_y(ny)
    rest = rows - more
    places = (
        [(0, 0)], [(0, rows)],
        [(1, 0)], [(1, rows), (3, 0)],
        [(4, 0), (2, 0)], [(2, more)],
        [(4, rest)], [(3, rest)],
    )
    return finish(g, (m, mx, my, nx, ny), places, taps, cp, chans, True)


def body_any(n_dp, layer_input, cotangent, momentum):
    chans = layer_input.shape[0]
    cp = -(-chans // 16) * 16
    taps = -(-TAPS // n_dp)
    x = jnp.pad(layer_input, ((0, cp - chans), (0, 0)))
    part = conv(x, cotangent, lambda: [list(range(n_dp))] * 2, n_dp, taps)[:2]
    grad = [lax.psum_scatter(p, "dp", scatter_dimension=0, tiled=True) for p in part]
    m = momentum_update(own_momentum(momentum, taps, cp), grad, taps, cp)
    gram = lax.psum(any_gram(m), ("dp", "shard"))
    rows = taps * cp
    full = [lax.all_gather(half, "dp", axis=0, tiled=True) for half in (m[:rows], m[rows:])]
    places = [[(half, r * rows)] for r in range(n_dp) for half in range(2)]
    return finish([gram], full, places, taps, cp, chans, False)


def solution(mesh):
    n_dp = mesh.shape["dp"]
    known = (n_dp, mesh.shape["shard"]) == (4, 8)
    return jax.shard_map(
        body_4x8 if known else functools.partial(body_any, n_dp),
        mesh=mesh,
        in_specs=(P("shard", "dp"), P("dp", None), P("shard", None)),
        out_specs=(P("shard", None), P("shard", None)),
        check_vma=False,
    )
```

```python
import functools

import jax
import jax.numpy as jnp
from jax import lax
from jax.experimental import pallas as pl
from jax.experimental.pallas import tpu as pltpu
from jax.sharding import PartitionSpec as P

HW = 32
ROWS = 10368
PW = HW + 2
LANE = 128
TAPS = 27
A1, B1, C1 = 3.4445, -4.775, 2.0315
F32 = jnp.float32
BF16 = jnp.bfloat16
VMEM = pl.BlockSpec(memory_space=pltpu.VMEM)
HBM = pl.BlockSpec(memory_space=pltpu.HBM)
BLOCKS = (((0, 1), (0, 2), (0, 3)), ((1, 2), (1, 3), (2, 3)))
PIECE = (136, 128)


def column(rows):
    return pl.BlockSpec((rows, LANE), lambda c: (0, c))


def params(mib=24):
    return pltpu.CompilerParams(vmem_limit_bytes=mib << 20)


def near(x):
    return pltpu.with_memory_space_constraint(x, pltpu.VMEM)


def far(x):
    return pltpu.with_memory_space_constraint(x, pltpu.HBM)


def pair(tile, p, lane):
    t, c = divmod(p, LANE)
    if c + 64 <= LANE:
        return jnp.where(lane < c + 32, tile(t), tile(t + 4))
    if c + 32 <= LANE:
        far = jnp.where(lane < c, tile(t + 5), tile(t))
        if c + 32 == LANE:
            return far
        return jnp.where(lane < c + 32, far, tile(t + 4))
    near = jnp.where(lane < c + 32 - LANE, tile(t + 1), tile(t + 5))
    return jnp.where(lane < c, near, tile(t))


def build_slab(d0, half, g, xs, tail, v, cp):
    lane = lax.broadcasted_iota(jnp.int32, (16, LANE), 1)
    last = xs.shape[1] // LANE
    rows = slice(16 * g, 16 * g + 16)

    def tile(t):
        return tail[rows, :] if t == last else xs[rows, LANE * t : LANE * t + LANE]

    for j in range(18):
        for kw in range(3):
            part = []
            for s1 in range(2):
                p = (d0 + half * s1) * PW * PW + PW * j + kw
                part.append(pltpu.roll(pair(tile, p, lane), (64 * s1 - p) % LANE, 1))
            r0 = (d0 * 3 + kw) * cp + 16 * g
            v[r0 : r0 + 16, LANE * j : LANE * j + LANE] = jnp.where(lane < 64, part[0], part[1])


def conv_part(d, half, taps, cp, qs, cot, v, outs):
    vox = HW * HW
    for c in range(2):
        lhs = []
        for q in qs[c]:
            for i in range(taps):
                t = jnp.minimum(q * taps + i, TAPS - 1)
                kd, kh, kw = t // 9, t // 3 % 3, t % 3
                r0 = pl.multiple_of(((d + kd) * 3 + kw) * cp, 16)
                lhs.append(v[pl.ds(r0, cp), pl.ds(pl.multiple_of(LANE * kh, LANE), 16 * LANE)])
        rhs = []
        for h in range(16):
            for s1 in range(2):
                for s0 in range(2):
                    r0 = (d + half * s1) * vox + (h + 16 * s0) * HW
                    rhs.append(cot[r0 : r0 + HW, 256 * c : 256 * c + 256])
        part = jnp.dot(jnp.concatenate(lhs, 0), jnp.concatenate(rhs, 0), preferred_element_type=F32)
        if d == 0:
            outs[c][...] = part
        else:
            outs[c][...] += part


def conv_kernel(depth, cp, taps, chunks, x_hbm, cot_hbm, *refs):
    outs = refs[:2]
    cot, v, xs, tail, xsem, csem = refs[2:]
    half = depth // 2
    ln = xs.shape[1]
    vox = HW * HW
    groups = [pl.ds(16 * g, 16) for g in range(cp // 16)]
    xcopies = [pltpu.make_async_copy(x_hbm.at[r], xs.at[r], xsem.at[g]) for g, r in enumerate(groups)]
    for copy in xcopies:
        copy.start()
    copies = []
    for i in range(depth):
        rows = pl.ds(i * vox, vox)
        copies.append(pltpu.make_async_copy(cot_hbm.at[rows], cot.at[rows], csem.at[i]))
    n = ln // LANE * LANE
    for g, copy in enumerate(xcopies):
        copy.wait()
        if g == 0:
            for d in range(half):
                for s1 in range(2):
                    copies[d + half * s1].start()
        if n < ln:
            tail[16 * g : 16 * g + 16, : ln - n] = xs[16 * g : 16 * g + 16, n:]
        for d0 in range(half + 2):
            build_slab(d0, half, g, xs, tail, v, cp)
    qs = chunks()
    for d in range(half):
        for s1 in range(2):
            copies[d + half * s1].wait()
        conv_part(d, half, taps, cp, qs, cot, v, outs)


def conv(x, cot, chunks, slots, taps):
    cp, ln = x.shape
    depth = cot.shape[0] // (HW * HW)
    return pl.pallas_call(
        functools.partial(conv_kernel, depth, cp, taps, chunks),
        out_shape=[pltpu.VMEM((slots * taps * cp, 256), F32)] * 2
        + [pltpu.VMEM(cot.shape, BF16), pltpu.VMEM((3 * (depth // 2 + 2) * cp, 18 * LANE), BF16)],
        in_specs=[HBM, HBM],
        out_specs=[VMEM] * 4,
        scratch_shapes=[
            pltpu.VMEM((cp, ln), BF16),
            pltpu.VMEM((cp, LANE), BF16),
            pltpu.SemaphoreType.DMA((cp // 16,)),
            pltpu.SemaphoreType.DMA((depth,)),
        ],
        compiler_params=params(),
        name="conv_first",
    )(far(x), far(cot))


def more_kernel(depth, cp, taps, chunks, cot, v, *outs):
    qs = chunks()
    for d in range(depth // 2):
        conv_part(d, depth // 2, taps, cp, qs, cot, v, outs)


def conv_more(cot, v, chunks, slots, taps, cp):
    depth = cot.shape[0] // (HW * HW)
    return pl.pallas_call(
        functools.partial(more_kernel, depth, cp, taps, chunks),
        out_shape=[pltpu.VMEM((slots * taps * cp, 256), F32)] * 2,
        in_specs=[VMEM] * 2,
        out_specs=[VMEM] * 2,
        compiler_params=params(),
        name="conv_more",
    )(near(cot), near(v))


def own_kernel(taps, cp, m_ref, o_ref):
    chans = m_ref.shape[0] // TAPS
    for i in range(taps):
        t = lax.axis_index("dp") * taps + i
        rows = m_ref[pl.ds(jnp.minimum(t, TAPS - 1), chans, stride=TAPS), :]
        o_ref[cp * i : cp * i + chans, :] = jnp.where(t < TAPS, rows, 0.0)
        if cp > chans:
            o_ref[cp * i + chans : cp * i + cp, :] = jnp.zeros((cp - chans, LANE), F32)


def own_momentum(momentum, taps, cp):
    return pl.pallas_call(
        functools.partial(own_kernel, taps, cp),
        out_shape=jax.ShapeDtypeStruct((taps * cp, momentum.shape[1]), F32),
        grid=(momentum.shape[1] // LANE,),
        in_specs=[column(momentum.shape[0])],
        out_specs=column(taps * cp),
        compiler_params=params(),
        name="own_momentum",
    )(momentum)


def split(x):
    hi = x.astype(BF16)
    return hi, (x - hi.astype(F32)).astype(BF16)


def dot_t(a, b):
    return lax.dot_general(a, b, (((0,), (0,)), ((), ())), preferred_element_type=F32)


def update(m, grad, taps, cp):
    tap = lax.axis_index("dp") * taps + lax.broadcasted_iota(jnp.int32, (taps * cp, 1), 0) // cp
    return jnp.where(tap < TAPS, 0.95 * m + grad, 0.0)


def update_kernel(taps, cp, m_ref, *refs):
    parts, out = refs[:-1], refs[-1]
    rows = taps * cp
    for c in range(2):
        grad = parts[c][...]
        for n in range(2 + c, len(parts), 2):
            grad = grad + parts[n][...]
        out[rows * c : rows * c + rows, :] = update(m_ref[:, 256 * c : 256 * c + 256], grad, taps, cp)


def momentum_update(own, parts, taps, cp):
    return pl.pallas_call(
        functools.partial(update_kernel, taps, cp),
        out_shape=pltpu.VMEM((2 * taps * cp, 256), F32),
        in_specs=[VMEM] * (1 + len(parts)),
        out_specs=VMEM,
        compiler_params=params(),
        name="momentum_update",
    )(near(own), *map(near, parts))


def upper_gram(m):
    hi, lo = split(m)
    out = []
    for i in range(4):
        a, b = slice(128 * i, 128 * i + 128), slice(128 * i, 512)
        width = 512 - 128 * i
        both = dot_t(hi[:, a], jnp.concatenate([hi[:, b], lo[:, b]], 1))
        out.append(both[:, :width] + (both[:, width:] + dot_t(lo[:, a], hi[:, b])))
    return out


def step_kernel(taps, cp, more, m_ref, *refs):
    m, fx, fy, keep, send = refs[-5:]
    update_kernel(taps, cp, m_ref, *refs[:-5], m)
    rows = taps * cp
    fx[...] = m[: rows + more, :]
    fy[...] = m[rows - more :, :]
    z, core = lax.axis_index("shard") // 2, lax.axis_index("shard") % 2
    gram = upper_gram(jnp.concatenate([m[:rows], m[rows:]], 1))
    row = lax.broadcasted_iota(jnp.int32, (128, 128), 0)
    col = lax.broadcasted_iota(jnp.int32, (128, 128), 1)
    for half in range(2):
        blocks = [gram[i][:, 128 * (j - i) : 128 * (j - i) + 128] for i, j in BLOCKS[half]]
        even, odd = gram[2 * half][:, :128], gram[2 * half + 1][:, :128]
        blocks.append(jnp.where(row <= col, even, odd))
        diag = jnp.where(row == col, odd, 0.0)
        for r in range(4):
            cut = slice(32 * r, 32 * r + 32)
            last = jnp.sum(diag[cut], axis=0, keepdims=True)
            last = jnp.where(row[:8] == 0, jnp.broadcast_to(last, (8, 128)), 0.0)
            piece = jnp.concatenate([block[cut] for block in blocks] + [last], 0)

            @pl.when(core == half)
            def _():
                keep[r ^ z] = piece

            @pl.when(core != half)
            def _():
                send[r ^ z] = piece


def step(own, parts, taps, cp, more):
    rows = taps * cp
    return pl.pallas_call(
        functools.partial(step_kernel, taps, cp, more),
        out_shape=[pltpu.VMEM((2 * rows, 256), F32)]
        + [pltpu.VMEM((rows + more, 256), F32)] * 2
        + [pltpu.VMEM((4,) + PIECE, F32)] * 2,
        in_specs=[VMEM] * (1 + len(parts)),
        out_specs=[VMEM] * 5,
        compiler_params=params(),
        name="momentum_gram",
    )(near(own), *map(near, parts))


def any_gram_kernel(m, g_ref):
    half = m.shape[0] // 2
    for i, rows in enumerate(upper_gram(jnp.concatenate([m[:half], m[half:]], 1))):
        g_ref[128 * i : 128 * i + 128, :] = jnp.zeros((128, 512), F32)
        g_ref[128 * i : 128 * i + 128, 128 * i :] = rows


def any_gram(m):
    return pl.pallas_call(
        any_gram_kernel,
        out_shape=jax.ShapeDtypeStruct((512, 512), F32),
        in_specs=[VMEM],
        out_specs=VMEM,
        compiler_params=params(),
        name="own_gram",
    )(near(m))


def second_kernel(more, m, mx, my, nx, ny):
    rows = m.shape[0] // 2
    nx[: rows - more, :] = m[rows + more :, :]
    nx[rows - more :, :] = my[more:, :]
    ny[: rows - more, :] = m[: rows - more, :]
    ny[rows - more :, :] = mx[:rows, :]


def second_step(m, mx, my, more):
    return pl.pallas_call(
        functools.partial(second_kernel, more),
        out_shape=[pltpu.VMEM((m.shape[0] - more, 256), F32)] * 2,
        in_specs=[VMEM] * 3,
        out_specs=[VMEM] * 2,
        compiler_params=params(),
        name="second_step",
    )(near(m), near(mx), near(my))


def mm(a, b):
    ah, al = a
    bh, bl = b
    d = functools.partial(jnp.dot, preferred_element_type=F32)
    return d(ah, bh) + (d(ah, bl) + d(al, bh))


def assemble(parts, g_ref, p_ref, d_ref):
    if len(parts) == 1:
        g_ref[...] = parts[0][...]
    else:
        z, core = lax.axis_index("shard") // 2, lax.axis_index("shard") % 2
        for n, part in enumerate(parts):
            which, r = n // 4, (2, 3, 1, 0)[n % 4]
            q = z ^ r
            for half in range(2):

                @pl.when(core ^ which == half)
                def _():
                    for k, (i, j) in enumerate(BLOCKS[half]):
                        rows = pl.ds(pl.multiple_of(128 * i + 32 * q, 32), 32)
                        g_ref[rows, 128 * j : 128 * j + 128] = part[32 * k : 32 * k + 32]
                    p_ref[half, pl.ds(pl.multiple_of(32 * q, 32), 32), :] = part[96:128]
                    d_ref[half, 8 * r : 8 * r + 8, :] = part[128:136]

        row = lax.broadcasted_iota(jnp.int32, (128, 128), 0)
        col = lax.broadcasted_iota(jnp.int32, (128, 128), 1)
        for half in range(2):
            up = p_ref[half]
            down = up.T
            odd = jnp.broadcast_to(jnp.sum(d_ref[half], axis=0, keepdims=True), (128, 128))
            a = 256 * half
            g_ref[a : a + 128, a : a + 128] = jnp.where(row <= col, up, down)
            g_ref[a + 128 : a + 256, a + 128 : a + 256] = jnp.where(row > col, up, jnp.where(row < col, down, odd))

    for i in range(4):
        for j in range(i + 1, 4):
            g_ref[128 * j : 128 * j + 128, 128 * i : 128 * i + 128] = g_ref[
                128 * i : 128 * i + 128, 128 * j : 128 * j + 128
            ].T


def tap_rows(places, parts, taps, cp, slot):
    out = []
    for n, base in places[slot]:
        ends = [b for m, b in sum(places, []) if m == n and b > base] + [parts[n].shape[0]]
        out += [(n, at) for at in range(base, min(ends), cp)]
    return out[:taps]


def row_cuts(rows):
    cuts = [min(rows, -(-rows * k // 128) * 8) for k in (0, 7, 13, 16)]
    return [(a, b) for a, b in zip(cuts, cuts[1:]) if b > a]


def finish_kernel(taps, cp, chans, known, places, count, *refs):
    parts, grams = refs[:count], refs[count:-11]
    new, out, g_ref, p_ref, d_ref, cols, hi, lo, acc, sem, osem = refs[-11:]
    copies = []

    def reorder(c):
        lanes = slice(LANE * (c % 2), LANE * (c % 2) + LANE)
        for r in range(len(places) // 2):
            rows = None
            for i, (n, at) in enumerate(tap_rows(places, parts, taps, cp, 2 * r + c // 2)):
                if not known and r * taps + i >= TAPS:
                    continue
                before, rows = rows, parts[n][at : at + chans, lanes]
                t = r * taps + i
                if known:
                    t = (lax.axis_index("dp") ^ r) * taps + i
                    if 3 * taps + i >= TAPS:
                        rows = jnp.where(t < TAPS, rows, before)
                        t = jnp.minimum(t, TAPS - 1)
                cols.at[c][pl.ds(t, chans, stride=TAPS), :] = rows
        hi[:, LANE * c : LANE * c + LANE], lo[:, LANE * c : LANE * c + LANE] = split(cols[c])
        copies.append(pltpu.make_async_copy(cols.at[c], new.at[:, pl.ds(LANE * c, LANE)], sem.at[c]))
        copies[-1].start()

    assemble(grams, g_ref, p_ref, d_ref)
    gram = g_ref[...]
    n = gram.shape[0]
    diag = lax.broadcasted_iota(jnp.int32, (n, n), 0) == lax.broadcasted_iota(jnp.int32, (n, n), 1)
    trace = jnp.sum(jnp.where(diag, gram, 0.0), keepdims=True)
    scale = 1.0 / (jnp.sqrt(trace) + 1e-07)
    g = gram * scale * scale
    gs = split(g)
    p1 = jnp.where(diag, A1, 0.0) + B1 * g + C1 * mm(gs, gs)
    reorder(0)
    p1s = split(p1)
    h = mm(gs, p1s)
    reorder(1)
    g2 = mm(split(h), p1s)
    reorder(2)
    g2s = split(g2)
    p2 = jnp.where(diag, A1, 0.0) + B1 * g2 + C1 * mm(g2s, g2s)
    reorder(3)
    qs = split(mm(p1s, split(p2)) * (scale * jnp.sqrt(F32(ROWS))))
    for k, (a, b) in enumerate(row_cuts(acc.shape[0])):
        acc[a:b, :] = mm((hi[a:b, :], lo[a:b, :]), qs)
        copies.append(pltpu.make_async_copy(acc.at[pl.ds(a, b - a)], out.at[pl.ds(a, b - a)], osem.at[k]))
        copies[-1].start()
    for copy in copies:
        copy.wait()


def finish(grams, parts, places, taps, cp, chans, known):
    rows = chans * TAPS
    return pl.pallas_call(
        functools.partial(finish_kernel, taps, cp, chans, known, list(places), len(parts)),
        out_shape=[jax.ShapeDtypeStruct((rows, 512), F32)] * 2,
        in_specs=[VMEM] * (len(grams) + len(parts)),
        out_specs=[HBM] * 2,
        scratch_shapes=[
            pltpu.VMEM((512, 512), F32),
            pltpu.VMEM((2, 128, 128), F32),
            pltpu.VMEM((2, 32, 128), F32),
            pltpu.VMEM((4, rows, LANE), F32),
            pltpu.VMEM((rows, 512), BF16),
            pltpu.VMEM((rows, 512), BF16),
            pltpu.VMEM((rows, 512), F32),
            pltpu.SemaphoreType.DMA((4,)),
            pltpu.SemaphoreType.DMA((3,)),
        ],
        compiler_params=params(),
        name="finish",
    )(*map(near, parts), *map(near, grams))


def swap(x, axis, size, bit):
    return lax.ppermute(x, axis, [(i, i ^ bit) for i in range(size)])


def over_x(x):
    return swap(x, "dp", 4, 1)


def over_y(x):
    return swap(x, "dp", 4, 2)


def over_core(x):
    return swap(x, "shard", 8, 1)


def over_z(x, r):
    return swap(x, "shard", 8, 2 * r)


def chunk_pair(a, b):
    def chunks():
        dp = lax.axis_index("dp")
        return [dp ^ a], [dp ^ b]

    return chunks


def body_4x8(layer_input, cotangent, momentum):
    chans = momentum.shape[0] // TAPS
    cp = layer_input.shape[0]
    taps = 7
    a3, b3, cot, v = conv(layer_input, cotangent, chunk_pair(3, 3), 1, taps)
    a3, b3 = over_x(a3), over_y(b3)
    a1, b1 = conv_more(cot, v, chunk_pair(1, 2), 1, taps, cp)
    a1, b1 = over_x(a1), over_y(b1)
    a2, b2 = conv_more(cot, v, chunk_pair(2, 1), 1, taps, cp)
    a2, b2 = over_y(a2 + a3), over_x(b2 + b3)
    a0, b0 = conv_more(cot, v, chunk_pair(0, 0), 1, taps, cp)
    own = own_momentum(momentum, taps, cp)
    rows = taps * cp
    more = 4 * cp
    m, fx, fy, keep, send = step(own, (a0, b0, a1, b1, a2, b2), taps, cp, more)
    mx, my = over_x(fx), over_y(fy)
    g = keep + over_core(send)
    za, zb, zc = [over_z(g[r], r) for r in (2, 3, 1)]
    g = (za + zb) + (zc + g[0])
    d3, d1, d2 = [swap(g, "dp", 4, r) for r in (3, 1, 2)]
    g = (d3 + d2) + (d1 + g)
    g = [over_z(g, r) for r in (2, 3, 1)] + [g]
    g = g + [over_core(x) for x in g]
    nx, ny = second_step(m, mx, my, more)
    nx, ny = over_x(nx), over_y(ny)
    rest = rows - more
    places = (
        [(0, 0)], [(0, rows)],
        [(1, 0)], [(1, rows), (3, 0)],
        [(4, 0), (2, 0)], [(2, more)],
        [(4, rest)], [(3, rest)],
    )
    return finish(g, (m, mx, my, nx, ny), places, taps, cp, chans, True)


def body_any(n_dp, layer_input, cotangent, momentum):
    chans = layer_input.shape[0]
    cp = -(-chans // 16) * 16
    taps = -(-TAPS // n_dp)
    x = jnp.pad(layer_input, ((0, cp - chans), (0, 0)))
    part = conv(x, cotangent, lambda: [list(range(n_dp))] * 2, n_dp, taps)[:2]
    grad = [lax.psum_scatter(p, "dp", scatter_dimension=0, tiled=True) for p in part]
    m = momentum_update(own_momentum(momentum, taps, cp), grad, taps, cp)
    gram = lax.psum(any_gram(m), ("dp", "shard"))
    rows = taps * cp
    full = [lax.all_gather(half, "dp", axis=0, tiled=True) for half in (m[:rows], m[rows:])]
    places = [[(half, r * rows)] for r in range(n_dp) for half in range(2)]
    return finish([gram], full, places, taps, cp, chans, False)


def solution(mesh):
    n_dp = mesh.shape["dp"]
    known = (n_dp, mesh.shape["shard"]) == (4, 8)
    return jax.shard_map(
        body_4x8 if known else functools.partial(body_any, n_dp),
        mesh=mesh,
        in_specs=(P("shard", "dp"), P("dp", None), P("shard", None)),
        out_specs=(P("shard", None), P("shard", None)),
        check_vma=False,
    )
```

```python
import functools

import jax
import jax.numpy as jnp
from jax import lax
from jax.experimental import pallas as pl
from jax.experimental.pallas import tpu as pltpu
from jax.sharding import PartitionSpec as P

HW = 32
ROWS = 10368
PW = HW + 2
LANE = 128
TAPS = 27
A1, B1, C1 = 3.4445, -4.775, 2.0315
F32 = jnp.float32
BF16 = jnp.bfloat16
VMEM = pl.BlockSpec(memory_space=pltpu.VMEM)
HBM = pl.BlockSpec(memory_space=pltpu.HBM)
BLOCKS = (((0, 1), (0, 2), (0, 3)), ((1, 2), (1, 3), (2, 3)))
PIECE = (136, 128)


def column(rows):
    return pl.BlockSpec((rows, LANE), lambda c: (0, c))


def params(mib=24):
    return pltpu.CompilerParams(vmem_limit_bytes=mib << 20)


def near(x):
    return pltpu.with_memory_space_constraint(x, pltpu.VMEM)


def far(x):
    return pltpu.with_memory_space_constraint(x, pltpu.HBM)


def pair(tile, p, lane):
    t, c = divmod(p, LANE)
    if c + 64 <= LANE:
        return jnp.where(lane < c + 32, tile(t), tile(t + 4))
    if c + 32 <= LANE:
        far = jnp.where(lane < c, tile(t + 5), tile(t))
        if c + 32 == LANE:
            return far
        return jnp.where(lane < c + 32, far, tile(t + 4))
    near = jnp.where(lane < c + 32 - LANE, tile(t + 1), tile(t + 5))
    return jnp.where(lane < c, near, tile(t))


def build_slab(d0, half, g, xs, tail, v, cp):
    lane = lax.broadcasted_iota(jnp.int32, (16, LANE), 1)
    last = xs.shape[1] // LANE
    rows = slice(16 * g, 16 * g + 16)

    def tile(t):
        return tail[rows, :] if t == last else xs[rows, LANE * t : LANE * t + LANE]

    for j in range(18):
        for kw in range(3):
            part = []
            for s1 in range(2):
                p = (d0 + half * s1) * PW * PW + PW * j + kw
                part.append(pltpu.roll(pair(tile, p, lane), (64 * s1 - p) % LANE, 1))
            r0 = (d0 * 3 + kw) * cp + 16 * g
            v[r0 : r0 + 16, LANE * j : LANE * j + LANE] = jnp.where(lane < 64, part[0], part[1])


def conv_part(steps, half, taps, cp, qs, cot, v, outs):
    vox = HW * HW
    for c in range(2):
        lhs, rhs = [], []
        for d in steps:
            rows = []
            for q in qs[c]:
                for i in range(taps):
                    t = jnp.minimum(q * taps + i, TAPS - 1)
                    kd, kh, kw = t // 9, t // 3 % 3, t % 3
                    r0 = pl.multiple_of(((d + kd) * 3 + kw) * cp, 16)
                    rows.append(v[pl.ds(r0, cp), pl.ds(pl.multiple_of(LANE * kh, LANE), 16 * LANE)])
            lhs.append(jnp.concatenate(rows, 0))
            for h in range(16):
                for s1 in range(2):
                    for s0 in range(2):
                        r0 = (d + half * s1) * vox + (h + 16 * s0) * HW
                        rhs.append(cot[r0 : r0 + HW, 256 * c : 256 * c + 256])
        part = jnp.dot(jnp.concatenate(lhs, 1), jnp.concatenate(rhs, 0), preferred_element_type=F32)
        if steps[0] == 0:
            outs[c][...] = part
        else:
            outs[c][...] += part


def conv_kernel(depth, cp, taps, chunks, x_hbm, cot_hbm, *refs):
    outs = refs[:2]
    cot, v, xs, tail, xsem, csem = refs[2:]
    half = depth // 2
    ln = xs.shape[1]
    vox = HW * HW
    groups = [pl.ds(16 * g, 16) for g in range(cp // 16)]
    xcopies = [pltpu.make_async_copy(x_hbm.at[r], xs.at[r], xsem.at[g]) for g, r in enumerate(groups)]
    for copy in xcopies:
        copy.start()
    copies = []
    for i in range(depth):
        rows = pl.ds(i * vox, vox)
        copies.append(pltpu.make_async_copy(cot_hbm.at[rows], cot.at[rows], csem.at[i]))
    n = ln // LANE * LANE
    for g, copy in enumerate(xcopies):
        copy.wait()
        if g == 0:
            for d in range(half):
                for s1 in range(2):
                    copies[d + half * s1].start()
        if n < ln:
            tail[16 * g : 16 * g + 16, : ln - n] = xs[16 * g : 16 * g + 16, n:]
        for d0 in range(half + 2):
            build_slab(d0, half, g, xs, tail, v, cp)
    qs = chunks()
    for d in range(0, half, 2):
        steps = list(range(d, min(d + 2, half)))
        for n in steps:
            for s1 in range(2):
                copies[n + half * s1].wait()
        conv_part(steps, half, taps, cp, qs, cot, v, outs)


def conv(x, cot, chunks, slots, taps):
    cp, ln = x.shape
    depth = cot.shape[0] // (HW * HW)
    return pl.pallas_call(
        functools.partial(conv_kernel, depth, cp, taps, chunks),
        out_shape=[pltpu.VMEM((slots * taps * cp, 256), F32)] * 2
        + [pltpu.VMEM(cot.shape, BF16), pltpu.VMEM((3 * (depth // 2 + 2) * cp, 18 * LANE), BF16)],
        in_specs=[HBM, HBM],
        out_specs=[VMEM] * 4,
        scratch_shapes=[
            pltpu.VMEM((cp, ln), BF16),
            pltpu.VMEM((cp, LANE), BF16),
            pltpu.SemaphoreType.DMA((cp // 16,)),
            pltpu.SemaphoreType.DMA((depth,)),
        ],
        compiler_params=params(),
        name="conv_first",
    )(far(x), far(cot))


def more_kernel(depth, cp, taps, chunks, cot, v, *outs):
    qs = chunks()
    half = depth // 2
    for d in range(0, half, 2):
        conv_part(list(range(d, min(d + 2, half))), half, taps, cp, qs, cot, v, outs)


def conv_more(cot, v, chunks, slots, taps, cp):
    depth = cot.shape[0] // (HW * HW)
    return pl.pallas_call(
        functools.partial(more_kernel, depth, cp, taps, chunks),
        out_shape=[pltpu.VMEM((slots * taps * cp, 256), F32)] * 2,
        in_specs=[VMEM] * 2,
        out_specs=[VMEM] * 2,
        compiler_params=params(),
        name="conv_more",
    )(near(cot), near(v))


def own_kernel(taps, cp, m_ref, o_ref):
    chans = m_ref.shape[0] // TAPS
    for i in range(taps):
        t = lax.axis_index("dp") * taps + i
        rows = m_ref[pl.ds(jnp.minimum(t, TAPS - 1), chans, stride=TAPS), :]
        o_ref[cp * i : cp * i + chans, :] = jnp.where(t < TAPS, rows, 0.0)
        if cp > chans:
            o_ref[cp * i + chans : cp * i + cp, :] = jnp.zeros((cp - chans, LANE), F32)


def own_momentum(momentum, taps, cp):
    return pl.pallas_call(
        functools.partial(own_kernel, taps, cp),
        out_shape=jax.ShapeDtypeStruct((taps * cp, momentum.shape[1]), F32),
        grid=(momentum.shape[1] // LANE,),
        in_specs=[column(momentum.shape[0])],
        out_specs=column(taps * cp),
        compiler_params=params(),
        name="own_momentum",
    )(momentum)


def split(x):
    hi = x.astype(BF16)
    return hi, (x - hi.astype(F32)).astype(BF16)


def dot_t(a, b):
    return lax.dot_general(a, b, (((0,), (0,)), ((), ())), preferred_element_type=F32)


def update(m, grad, taps, cp):
    tap = lax.axis_index("dp") * taps + lax.broadcasted_iota(jnp.int32, (taps * cp, 1), 0) // cp
    return jnp.where(tap < TAPS, 0.95 * m + grad, 0.0)


def update_kernel(taps, cp, m_ref, *refs):
    parts, out = refs[:-1], refs[-1]
    rows = taps * cp
    for c in range(2):
        grad = parts[c][...]
        for n in range(2 + c, len(parts), 2):
            grad = grad + parts[n][...]
        out[rows * c : rows * c + rows, :] = update(m_ref[:, 256 * c : 256 * c + 256], grad, taps, cp)


def momentum_update(own, parts, taps, cp):
    return pl.pallas_call(
        functools.partial(update_kernel, taps, cp),
        out_shape=pltpu.VMEM((2 * taps * cp, 256), F32),
        in_specs=[VMEM] * (1 + len(parts)),
        out_specs=VMEM,
        compiler_params=params(),
        name="momentum_update",
    )(near(own), *map(near, parts))


def upper_gram(m):
    hi, lo = split(m)
    out = []
    for i in range(4):
        a, b = slice(128 * i, 128 * i + 128), slice(128 * i, 512)
        width = 512 - 128 * i
        both = dot_t(hi[:, a], jnp.concatenate([hi[:, b], lo[:, b]], 1))
        out.append(both[:, :width] + (both[:, width:] + dot_t(lo[:, a], hi[:, b])))
    return out


def step_kernel(taps, cp, more, m_ref, *refs):
    m, fx, fy, keep, send = refs[-5:]
    update_kernel(taps, cp, m_ref, *refs[:-5], m)
    rows = taps * cp
    fx[...] = m[: rows + more, :]
    fy[...] = m[rows - more :, :]
    z, core = lax.axis_index("shard") // 2, lax.axis_index("shard") % 2
    gram = upper_gram(jnp.concatenate([m[:rows], m[rows:]], 1))
    row = lax.broadcasted_iota(jnp.int32, (128, 128), 0)
    col = lax.broadcasted_iota(jnp.int32, (128, 128), 1)
    for half in range(2):
        blocks = [gram[i][:, 128 * (j - i) : 128 * (j - i) + 128] for i, j in BLOCKS[half]]
        even, odd = gram[2 * half][:, :128], gram[2 * half + 1][:, :128]
        blocks.append(jnp.where(row <= col, even, odd))
        diag = jnp.where(row == col, odd, 0.0)
        for r in range(4):
            cut = slice(32 * r, 32 * r + 32)
            last = jnp.sum(diag[cut], axis=0, keepdims=True)
            last = jnp.where(row[:8] == 0, jnp.broadcast_to(last, (8, 128)), 0.0)
            piece = jnp.concatenate([block[cut] for block in blocks] + [last], 0)

            @pl.when(core == half)
            def _():
                keep[r ^ z] = piece

            @pl.when(core != half)
            def _():
                send[r ^ z] = piece


def step(own, parts, taps, cp, more):
    rows = taps * cp
    return pl.pallas_call(
        functools.partial(step_kernel, taps, cp, more),
        out_shape=[pltpu.VMEM((2 * rows, 256), F32)]
        + [pltpu.VMEM((rows + more, 256), F32)] * 2
        + [pltpu.VMEM((4,) + PIECE, F32)] * 2,
        in_specs=[VMEM] * (1 + len(parts)),
        out_specs=[VMEM] * 5,
        compiler_params=params(),
        name="momentum_gram",
    )(near(own), *map(near, parts))


def any_gram_kernel(m, g_ref):
    half = m.shape[0] // 2
    for i, rows in enumerate(upper_gram(jnp.concatenate([m[:half], m[half:]], 1))):
        g_ref[128 * i : 128 * i + 128, :] = jnp.zeros((128, 512), F32)
        g_ref[128 * i : 128 * i + 128, 128 * i :] = rows


def any_gram(m):
    return pl.pallas_call(
        any_gram_kernel,
        out_shape=jax.ShapeDtypeStruct((512, 512), F32),
        in_specs=[VMEM],
        out_specs=VMEM,
        compiler_params=params(),
        name="own_gram",
    )(near(m))


def second_kernel(more, m, mx, my, nx, ny):
    rows = m.shape[0] // 2
    nx[: rows - more, :] = m[rows + more :, :]
    nx[rows - more :, :] = my[more:, :]
    ny[: rows - more, :] = m[: rows - more, :]
    ny[rows - more :, :] = mx[:rows, :]


def second_step(m, mx, my, more):
    return pl.pallas_call(
        functools.partial(second_kernel, more),
        out_shape=[pltpu.VMEM((m.shape[0] - more, 256), F32)] * 2,
        in_specs=[VMEM] * 3,
        out_specs=[VMEM] * 2,
        compiler_params=params(),
        name="second_step",
    )(near(m), near(mx), near(my))


def mm(a, b):
    ah, al = a
    bh, bl = b
    d = functools.partial(jnp.dot, preferred_element_type=F32)
    return d(ah, bh) + (d(ah, bl) + d(al, bh))


def assemble(parts, g_ref, p_ref, d_ref):
    if len(parts) == 1:
        g_ref[...] = parts[0][...]
    else:
        z, core = lax.axis_index("shard") // 2, lax.axis_index("shard") % 2
        for n, part in enumerate(parts):
            which, r = n // 4, (2, 3, 1, 0)[n % 4]
            q = z ^ r
            for half in range(2):

                @pl.when(core ^ which == half)
                def _():
                    for k, (i, j) in enumerate(BLOCKS[half]):
                        rows = pl.ds(pl.multiple_of(128 * i + 32 * q, 32), 32)
                        g_ref[rows, 128 * j : 128 * j + 128] = part[32 * k : 32 * k + 32]
                    p_ref[half, pl.ds(pl.multiple_of(32 * q, 32), 32), :] = part[96:128]
                    d_ref[half, 8 * r : 8 * r + 8, :] = part[128:136]

        row = lax.broadcasted_iota(jnp.int32, (128, 128), 0)
        col = lax.broadcasted_iota(jnp.int32, (128, 128), 1)
        for half in range(2):
            up = p_ref[half]
            down = up.T
            odd = jnp.broadcast_to(jnp.sum(d_ref[half], axis=0, keepdims=True), (128, 128))
            a = 256 * half
            g_ref[a : a + 128, a : a + 128] = jnp.where(row <= col, up, down)
            g_ref[a + 128 : a + 256, a + 128 : a + 256] = jnp.where(row > col, up, jnp.where(row < col, down, odd))

    for i in range(4):
        for j in range(i + 1, 4):
            g_ref[128 * j : 128 * j + 128, 128 * i : 128 * i + 128] = g_ref[
                128 * i : 128 * i + 128, 128 * j : 128 * j + 128
            ].T


def tap_rows(places, parts, taps, cp, slot):
    out = []
    for n, base in places[slot]:
        ends = [b for m, b in sum(places, []) if m == n and b > base] + [parts[n].shape[0]]
        out += [(n, at) for at in range(base, min(ends), cp)]
    return out[:taps]


def row_cuts(rows):
    cuts = [min(rows, -(-rows * k // 128) * 8) for k in (0, 7, 13, 16)]
    return [(a, b) for a, b in zip(cuts, cuts[1:]) if b > a]


def finish_kernel(taps, cp, chans, known, places, count, *refs):
    parts, grams = refs[:count], refs[count:-11]
    new, out, g_ref, p_ref, d_ref, cols, hi, lo, acc, sem, osem = refs[-11:]
    copies = []

    def reorder(c):
        lanes = slice(LANE * (c % 2), LANE * (c % 2) + LANE)
        for r in range(len(places) // 2):
            rows = None
            for i, (n, at) in enumerate(tap_rows(places, parts, taps, cp, 2 * r + c // 2)):
                if not known and r * taps + i >= TAPS:
                    continue
                before, rows = rows, parts[n][at : at + chans, lanes]
                t = r * taps + i
                if known:
                    t = (lax.axis_index("dp") ^ r) * taps + i
                    if 3 * taps + i >= TAPS:
                        rows = jnp.where(t < TAPS, rows, before)
                        t = jnp.minimum(t, TAPS - 1)
                cols.at[c][pl.ds(t, chans, stride=TAPS), :] = rows
        hi[:, LANE * c : LANE * c + LANE], lo[:, LANE * c : LANE * c + LANE] = split(cols[c])
        copies.append(pltpu.make_async_copy(cols.at[c], new.at[:, pl.ds(LANE * c, LANE)], sem.at[c]))
        copies[-1].start()

    assemble(grams, g_ref, p_ref, d_ref)
    gram = g_ref[...]
    n = gram.shape[0]
    diag = lax.broadcasted_iota(jnp.int32, (n, n), 0) == lax.broadcasted_iota(jnp.int32, (n, n), 1)
    trace = jnp.sum(jnp.where(diag, gram, 0.0), keepdims=True)
    scale = 1.0 / (jnp.sqrt(trace) + 1e-07)
    g = gram * scale * scale
    gs = split(g)
    p1 = jnp.where(diag, A1, 0.0) + B1 * g + C1 * mm(gs, gs)
    reorder(0)
    p1s = split(p1)
    h = mm(gs, p1s)
    reorder(1)
    g2 = mm(split(h), p1s)
    reorder(2)
    g2s = split(g2)
    p2 = jnp.where(diag, A1, 0.0) + B1 * g2 + C1 * mm(g2s, g2s)
    reorder(3)
    qs = split(mm(p1s, split(p2)) * (scale * jnp.sqrt(F32(ROWS))))
    for k, (a, b) in enumerate(row_cuts(acc.shape[0])):
        acc[a:b, :] = mm((hi[a:b, :], lo[a:b, :]), qs)
        copies.append(pltpu.make_async_copy(acc.at[pl.ds(a, b - a)], out.at[pl.ds(a, b - a)], osem.at[k]))
        copies[-1].start()
    for copy in copies:
        copy.wait()


def finish(grams, parts, places, taps, cp, chans, known):
    rows = chans * TAPS
    return pl.pallas_call(
        functools.partial(finish_kernel, taps, cp, chans, known, list(places), len(parts)),
        out_shape=[jax.ShapeDtypeStruct((rows, 512), F32)] * 2,
        in_specs=[VMEM] * (len(grams) + len(parts)),
        out_specs=[HBM] * 2,
        scratch_shapes=[
            pltpu.VMEM((512, 512), F32),
            pltpu.VMEM((2, 128, 128), F32),
            pltpu.VMEM((2, 32, 128), F32),
            pltpu.VMEM((4, rows, LANE), F32),
            pltpu.VMEM((rows, 512), BF16),
            pltpu.VMEM((rows, 512), BF16),
            pltpu.VMEM((rows, 512), F32),
            pltpu.SemaphoreType.DMA((4,)),
            pltpu.SemaphoreType.DMA((3,)),
        ],
        compiler_params=params(),
        name="finish",
    )(*map(near, parts), *map(near, grams))


def swap(x, axis, size, bit):
    return lax.ppermute(x, axis, [(i, i ^ bit) for i in range(size)])


def over_x(x):
    return swap(x, "dp", 4, 1)


def over_y(x):
    return swap(x, "dp", 4, 2)


def over_core(x):
    return swap(x, "shard", 8, 1)


def over_z(x, r):
    return swap(x, "shard", 8, 2 * r)


def chunk_pair(a, b):
    def chunks():
        dp = lax.axis_index("dp")
        return [dp ^ a], [dp ^ b]

    return chunks


def body_4x8(layer_input, cotangent, momentum):
    chans = momentum.shape[0] // TAPS
    cp = layer_input.shape[0]
    taps = 7
    a3, b3, cot, v = conv(layer_input, cotangent, chunk_pair(3, 3), 1, taps)
    a3, b3 = over_x(a3), over_y(b3)
    a1, b1 = conv_more(cot, v, chunk_pair(1, 2), 1, taps, cp)
    a1, b1 = over_x(a1), over_y(b1)
    a2, b2 = conv_more(cot, v, chunk_pair(2, 1), 1, taps, cp)
    a2, b2 = over_y(a2 + a3), over_x(b2 + b3)
    a0, b0 = conv_more(cot, v, chunk_pair(0, 0), 1, taps, cp)
    own = own_momentum(momentum, taps, cp)
    rows = taps * cp
    more = 4 * cp
    m, fx, fy, keep, send = step(own, (a0, b0, a1, b1, a2, b2), taps, cp, more)
    mx, my = over_x(fx), over_y(fy)
    g = keep + over_core(send)
    za, zb, zc = [over_z(g[r], r) for r in (2, 3, 1)]
    g = (za + zb) + (zc + g[0])
    d3, d1, d2 = [swap(g, "dp", 4, r) for r in (3, 1, 2)]
    g = (d3 + d2) + (d1 + g)
    g = [over_z(g, r) for r in (2, 3, 1)] + [g]
    g = g + [over_core(x) for x in g]
    nx, ny = second_step(m, mx, my, more)
    nx, ny = over_x(nx), over_y(ny)
    rest = rows - more
    places = (
        [(0, 0)], [(0, rows)],
        [(1, 0)], [(1, rows), (3, 0)],
        [(4, 0), (2, 0)], [(2, more)],
        [(4, rest)], [(3, rest)],
    )
    return finish(g, (m, mx, my, nx, ny), places, taps, cp, chans, True)


def body_any(n_dp, layer_input, cotangent, momentum):
    chans = layer_input.shape[0]
    cp = -(-chans // 16) * 16
    taps = -(-TAPS // n_dp)
    x = jnp.pad(layer_input, ((0, cp - chans), (0, 0)))
    part = conv(x, cotangent, lambda: [list(range(n_dp))] * 2, n_dp, taps)[:2]
    grad = [lax.psum_scatter(p, "dp", scatter_dimension=0, tiled=True) for p in part]
    m = momentum_update(own_momentum(momentum, taps, cp), grad, taps, cp)
    gram = lax.psum(any_gram(m), ("dp", "shard"))
    rows = taps * cp
    full = [lax.all_gather(half, "dp", axis=0, tiled=True) for half in (m[:rows], m[rows:])]
    places = [[(half, r * rows)] for r in range(n_dp) for half in range(2)]
    return finish([gram], full, places, taps, cp, chans, False)


def solution(mesh):
    n_dp = mesh.shape["dp"]
    known = (n_dp, mesh.shape["shard"]) == (4, 8)
    return jax.shard_map(
        body_4x8 if known else functools.partial(body_any, n_dp),
        mesh=mesh,
        in_specs=(P("shard", "dp"), P("dp", None), P("shard", None)),
        out_specs=(P("shard", None), P("shard", None)),
        check_vma=False,
    )
```
